256 devices in a mesh: seq: 32 (over x_hi, z, core), tp: 8 (over x_lo, y).
Axes of the slice: x: 4 (x_hi: 2, x_lo: 2; x = x_hi * 2 + x_lo), y: 4, z: 8, core: 2. Of those that a mesh axis runs over, the one named last changes fastest.
Arguments:
- tokens: bfloat16 [16384, 1536], P(('seq', 'tp')), may hold values from -3 to 3
- segment_ids: int32 [16384], P(('seq', 'tp')), may hold values from 0 to 5, never falling along the last dimension, each value on 1 to 4096 neighbouring positions
- routes: int32 [16384, 4], P(('seq', 'tp')), may hold values from 0 to 31, all different within a row; in each aligned block of 512 rows (0 to 511, 512 to 1023, ...) at most 128 rows name the same one
- attn_gain: float32 [1536], replicated, may hold values from 0.5 to 1.5
- w_query: bfloat16 [1536, 1024], P(None, 'tp'), may hold values from -9 to 9
- w_key: bfloat16 [1536, 256], replicated, may hold values from -0.5 to 0.5
- w_value: bfloat16 [1536, 256], replicated, may hold values from -2.5 to 2.5
- w_out: bfloat16 [1024, 1536], P('tp'), may hold values from -0.1875 to 0.1875
- moe_gain: float32 [1536], replicated, may hold values from 0.5 to 1.5
- w_router: bfloat16 [1536, 32], replicated, may hold values from -30 to 30
- w_gate: bfloat16 [32, 1536, 768], P('seq'), may hold values from -0.15625 to 0.15625
- w_up: bfloat16 [32, 1536, 768], P('seq'), may hold values from -0.15625 to 0.15625
- w_down: bfloat16 [32, 768, 1536], P('seq'), may hold values from -0.21875 to 0.21875
Outputs:
- layer_out: bfloat16 [16384, 1536], P(('seq', 'tp'))
- kv_cache: bfloat16 [2, 2, 16384, 128], P(None, None, ('seq', 'tp'))
The draws below stay inside these ranges and needn't reach their ends.
Inputs may be any that keep to these rules, and one draw needn't show every extreme that they name: `segment_ids`: numbers never fall along the stream; every prompt has at most 4096 tokens and one has exactly 4096. `routes`: A token names 4 different experts. In each aligned block of 512 tokens no expert is named by more than 128 tokens, a bound that some block reaches.
All inputs are finite; a program needn't handle non-finite values.
Results may differ from the reference program's by a relative error of at most 0.018.
Values may be sent and summed in bfloat16 or wider, within the bound.
A program may use at most 128 MiB of HBM per device.

```python
import math
import jax
import jax.numpy as jnp
import numpy as np
from jax import lax

D = 1536
HD = 128
QH = 8
KVH = 2
FF_E = 768
TOP = 4
TOK_SEQ = 512
E = 32
TOKENS = 16384
MAXLEN = 4096
NSEG = 6
CAP = 128
N_SEQ = 32


def key_columns(key):
    base = jax.random.truncated_normal(jax.random.fold_in(key, 11), -4.0, 4.0, (D, KVH * HD), jnp.float32)
    return base / math.sqrt(D)


def draw_w_key(key, part):
    return key_columns(key).astype(jnp.bfloat16)


def draw_w_query(key, part):
    noise = jax.random.truncated_normal(jax.random.fold_in(key, 12), -4.0, 4.0, (D, QH * HD), jnp.float32) / math.sqrt(D)
    return noise.astype(jnp.bfloat16)


def draw_w_router(key, part):
    base = jax.random.truncated_normal(jax.random.fold_in(key, 21), -4.0, 4.0, (D, E), jnp.float32)
    column_scale = jnp.full((E,), 3.0, jnp.float32)
    return (base * column_scale[None, :] / math.sqrt(D)).astype(jnp.bfloat16)


def levels(stream_key, extent, split, least, largest):
    level = 1.0
    for dim, blocks in split:
        steps = jax.random.uniform(jax.random.fold_in(jax.random.fold_in(stream_key, 6), dim), (blocks,), jnp.float32, least / len(split), largest / len(split))
        level = level * jnp.repeat(jnp.exp(steps), extent[dim] // blocks).reshape((-1,) + (1,) * (len(extent) - 1 - dim))
    return level


def split_up(number_of, total, limit, skew):
    weights = [(1 << 20) // math.isqrt(standing ** skew) + 1 for standing in range(2, number_of + 1)]
    spare, given = total - limit - (number_of - 1), [1] * (number_of - 1)
    while spare > 0:
        free = [i for i in range(number_of - 1) if given[i] < limit]
        pool, left = sum([weights[i] for i in free]), spare
        for i in free:
            extra = min(limit - given[i], max(1, left * weights[i] // pool), spare)
            given[i] = given[i] + extra
            spare = spare - extra
    return np.array([limit] + given)


def uneven(stream_key, number_of, total, limit, lean):
    if number_of == 2:
        one = jax.random.randint(stream_key, (), max(1, total - limit), min(limit, total - 1) + 1)
        return jnp.stack([one, total - one])
    lengths = jnp.asarray(split_up(number_of, total, limit, lean), jnp.int32)
    pairs = (number_of - 1) // 2
    source_of, receiver = lengths[1:1 + 2 * pairs:2], lengths[2:2 + 2 * pairs:2]
    room = jnp.minimum(source_of - 1, limit - receiver)
    passed = jax.random.randint(jax.random.fold_in(stream_key, 1), (pairs,), 0, 1 << 20) % (room + 1)
    lengths = lengths.at[1:1 + 2 * pairs:2].set(source_of - passed).at[2:2 + 2 * pairs:2].set(receiver + passed)
    return lengths[jax.random.permutation(jax.random.fold_in(stream_key, 2), number_of)]


def shared_out(own_key, own, number, rows, number_of, top, reach, skew):
    sequence = jax.random.permutation(own_key, number_of)
    packed, common = shares(number_of, rows * top, reach, skew, True), shares(number_of, rows * top, reach, skew, False)
    places = jnp.arange(number_of)

    def named(sizes, rotation):
        used = int((sizes > 0).sum())
        fixed = max(1, used // 4)
        shifted = fixed + (places - fixed + rotation * (used - fixed)) % max(1, number_of - fixed)
        return jnp.zeros((number_of,), jnp.int32).at[sequence[jnp.where(places < fixed, places, shifted)]].set(jnp.asarray(sizes, jnp.int32))

    sizes = jnp.where(number % 4 == 0, named(packed, number // 4), named(common, number - number // 4 - 1))
    mixed = jax.random.permutation(jax.random.fold_in(own, 3), number_of)
    donor, sink = mixed[0:number_of // 2 * 2:2], mixed[1:number_of // 2 * 2:2]
    slack = jnp.minimum(sizes[donor] - 1, reach - sizes[sink]) // 2
    slack = jnp.where((donor == sequence[0]) | (sink == sequence[0]) | (sizes[sink] == 0), 0, jnp.maximum(slack, 0))
    shifted = jax.random.randint(jax.random.fold_in(own, 4), (number_of // 2,), 0, 1 << 20) % (slack + 1)
    sizes = sizes.at[donor].add(-shifted).at[sink].add(shifted)
    items = jnp.searchsorted(jnp.cumsum(sizes), jnp.arange(rows * top), side="right").astype(jnp.int32)
    table = items.reshape(top, rows).T
    table = table[jax.random.permutation(jax.random.fold_in(own, 1), rows)]
    rotation = jax.random.randint(jax.random.fold_in(own, 2), (rows, 1), 0, top)
    return jnp.take_along_axis(table, (jnp.arange(top)[None, :] + rotation) % top, axis=1)


def shares(number_of, total, most, lean, full):
    portions = [(1 << 20) // math.isqrt(grade ** lean) + 1 for grade in range(1, number_of + 1)]
    largest = most if full else min(most, max(-(-total // number_of), total * portions[0] // sum(portions)))
    least = 1 if total - largest >= number_of - 1 else 0
    holding, rest = [largest] + [least] * (number_of - 1), total - largest - least * (number_of - 1)
    while rest > 0:
        free = [i for i in range(1, number_of) if holding[i] < largest] or [i for i in range(1, number_of) if holding[i] < most]
        pool, budget = sum([portions[i] for i in free]), rest
        for i in free:
            more = min(most - holding[i], max(1, budget * portions[i] // pool), rest)
            holding[i] = holding[i] + more
            rest = rest - more
    return np.array(holding)


def normal_values(key, dims, scale, bound, pieces=(), kind=jnp.bfloat16):
    level = levels(key, dims, pieces, -0.22, 0.18) if pieces else 1.0
    result = jax.random.normal(key, dims, jnp.float32) * scale * level
    return jnp.minimum(jnp.maximum(result, -bound), bound).astype(kind)


def setup_inputs(seed: int = 0) -> dict:
    streams_of = jax.random.split(jax.random.key(seed), 14)
    tokens = normal_values(streams_of[0], (TOKENS, D), 0.5, 3.0, ((0, 256),))
    segment_ids = jnp.searchsorted(jnp.cumsum(uneven(streams_of[1], NSEG, TOKENS, MAXLEN, 2)), jnp.arange(TOKENS), side="right").astype(jnp.int32)
    routes_keys = jax.random.split(jax.random.fold_in(streams_of[2], 1), TOKENS // TOK_SEQ)
    routes_turns = jax.random.permutation(jax.random.fold_in(streams_of[2], 3), TOKENS // TOK_SEQ)
    routes = jax.vmap(lambda own, number: shared_out(jax.random.fold_in(streams_of[2], 2), own, number, TOK_SEQ, E, TOP, CAP, 2))(routes_keys, routes_turns).reshape((TOKENS, TOP))
    attn_gain = jnp.clip(1.0 + 0.1 * jax.random.normal(streams_of[3], (D,), jnp.float32), 0.5, 1.5)
    w_query = draw_w_query(jax.random.fold_in(streams_of[13], 71), 0)
    w_key = draw_w_key(jax.random.fold_in(streams_of[13], 71), 0)
    w_value = normal_values(streams_of[6], (D, KVH * HD), (max(1, D // 256)) ** -0.5, 2.5)
    w_out = normal_values(streams_of[7], (QH * HD, D), (QH * HD) ** -0.5, 0.1875, ((0, 8),))
    moe_gain = jnp.clip(1.0 + 0.1 * jax.random.normal(streams_of[8], (D,), jnp.float32), 0.5, 1.5)
    w_router = draw_w_router(jax.random.fold_in(streams_of[13], 71), 0)
    w_gate = normal_values(streams_of[10], (E, D, FF_E), D ** -0.5, 0.15625, ((0, 32),))
    w_up = normal_values(streams_of[11], (E, D, FF_E), D ** -0.5, 0.15625, ((0, 32),))
    w_down = normal_values(streams_of[12], (E, FF_E, D), FF_E ** -0.5, 0.21875, ((0, 32),))
    return {"tokens": tokens, "segment_ids": segment_ids, "routes": routes, "attn_gain": attn_gain, "w_query": w_query, "w_key": w_key, "w_value": w_value, "w_out": w_out, "moe_gain": moe_gain, "w_router": w_router, "w_gate": w_gate, "w_up": w_up, "w_down": w_down}


ROTARY = 1000000.0

def rms_rows(values_in, gain):
    wide = values_in.astype(jnp.float32)
    scale = lax.rsqrt(lax.optimization_barrier(jnp.mean(wide * wide, axis=-1, keepdims=True)) + 1e-06)
    return wide * scale * gain

def rotate(matrix, position):
    count = matrix.shape[0]
    shaped = matrix.reshape(count, -1, HD)
    half = HD // 2
    inverse = ROTARY ** (-(jnp.arange(half, dtype=jnp.float32) * 2.0 / HD))
    angle = position.astype(jnp.float32)[:, None] * inverse[None, :]
    cosine = jnp.cos(angle)[:, None, :]
    sine = jnp.sin(angle)[:, None, :]
    first = shaped[..., :half]
    second = shaped[..., half:]
    turned = jnp.concatenate([first * cosine - second * sine, second * cosine + first * sine], axis=-1)
    return turned.reshape(count, -1)

def reference(tokens, segment_ids, routes, attn_gain, w_query, w_key, w_value, w_out, moe_gain, w_router, w_gate, w_up, w_down):
    index = jnp.arange(TOKENS, dtype=jnp.int32)
    normed = rms_rows(tokens, attn_gain).astype(jnp.bfloat16)
    labels = jnp.arange(NSEG, dtype=jnp.int32)
    same = segment_ids[:, None] == labels[None, :]
    firsts = lax.optimization_barrier(jnp.min(jnp.where(same, index[:, None], TOKENS), axis=0))
    starts = lax.optimization_barrier(jnp.sum(jnp.where(same, firsts[None, :], 0), axis=1)).astype(jnp.int32)
    position = index - starts
    query = rotate(jnp.dot(normed, w_query, preferred_element_type=jnp.float32), position).astype(jnp.bfloat16)
    keys = rotate(jnp.dot(normed, w_key, preferred_element_type=jnp.float32), position).astype(jnp.bfloat16)
    values = jnp.dot(normed, w_value, preferred_element_type=jnp.float32).astype(jnp.bfloat16)
    keys_by_head = keys.reshape(TOKENS, KVH, HD)
    values_by_head = values.reshape(TOKENS, KVH, HD)
    kv_cache = jnp.stack([jnp.transpose(keys_by_head, (1, 0, 2)), jnp.transpose(values_by_head, (1, 0, 2))])
    group = QH // KVH
    block = TOK_SEQ
    window = min(TOKENS, MAXLEN + block)
    scale = 1.0 / math.sqrt(HD)

    def attend_block(block_id):
        q_first = (block_id * block).astype(jnp.int32)
        k_first = jnp.maximum(q_first + block - window, 0).astype(jnp.int32)
        q_rows = lax.dynamic_slice_in_dim(query, q_first, block, 0).reshape(block, KVH, group, HD).astype(jnp.float32)
        k_rows = lax.dynamic_slice_in_dim(keys_by_head, k_first, window, 0).astype(jnp.float32)
        v_rows = lax.dynamic_slice_in_dim(values_by_head, k_first, window, 0).astype(jnp.float32)
        q_segs = lax.dynamic_slice_in_dim(segment_ids, q_first, block, 0)
        k_segs = lax.dynamic_slice_in_dim(segment_ids, k_first, window, 0)
        q_index = q_first + jnp.arange(block, dtype=jnp.int32)
        k_index = k_first + jnp.arange(window, dtype=jnp.int32)
        scores = jnp.einsum('qcgd,kcd->cgqk', q_rows, k_rows) * scale
        allowed = (k_index[None, :] <= q_index[:, None]) & (k_segs[None, :] == q_segs[:, None])
        masked = jnp.where(allowed, scores, -1e+30)
        peak = lax.optimization_barrier(jnp.max(masked, axis=-1, keepdims=True))
        expd = jnp.where(allowed, jnp.exp(masked - peak), 0.0)
        denom = lax.optimization_barrier(jnp.sum(expd, axis=-1))
        probs = lax.optimization_barrier(expd.astype(jnp.bfloat16)).astype(jnp.float32)
        mixed = jnp.einsum('cgqk,kcd->cgqd', probs, v_rows) / denom[..., None]
        return jnp.transpose(mixed, (2, 0, 1, 3)).reshape(block, QH * HD).astype(jnp.bfloat16)
    attention = lax.map(attend_block, jnp.arange(TOKENS // block, dtype=jnp.int32)).reshape(TOKENS, QH * HD)
    resid = tokens.astype(jnp.float32) + jnp.dot(attention, w_out, preferred_element_type=jnp.float32)
    moe_in = rms_rows(resid, moe_gain).astype(jnp.bfloat16)
    logits = jnp.dot(moe_in, w_router, preferred_element_type=jnp.float32)
    expert_ids = jnp.arange(E, dtype=jnp.int32)
    chosen = lax.optimization_barrier(jnp.sum(jnp.where(routes[:, :, None] == expert_ids[None, None, :], logits[:, None, :], 0.0), axis=-1))
    gates = jax.nn.softmax(chosen, axis=-1).astype(jnp.bfloat16)
    row_limit = N_SEQ * CAP

    def one_expert(accum, inputs):
        expert, gate_w, up_w, down_w = inputs
        hit = routes == expert
        routed = jnp.any(hit, axis=1)
        weight = lax.optimization_barrier(jnp.sum(jnp.where(hit, gates.astype(jnp.float32), 0.0), axis=1))
        picked = jnp.nonzero(routed, size=row_limit, fill_value=0)[0].astype(jnp.int32)
        valid = jnp.arange(row_limit, dtype=jnp.int32) < jnp.sum(routed.astype(jnp.int32))
        rows_in = moe_in[picked]
        gate_out = jnp.dot(rows_in, gate_w, preferred_element_type=jnp.float32)
        up_out = jnp.dot(rows_in, up_w, preferred_element_type=jnp.float32)
        active = (jax.nn.relu(gate_out) * up_out).astype(jnp.bfloat16)
        down_out = jnp.dot(active, down_w, preferred_element_type=jnp.float32) * weight[picked][:, None]
        contribution = down_out.astype(jnp.bfloat16).astype(jnp.float32)
        contribution = jnp.where(valid[:, None], contribution, 0.0)
        return (accum.at[picked].add(contribution), None)
    total, _ = lax.scan(one_expert, jnp.zeros((TOKENS, D), jnp.float32), (expert_ids, w_gate, w_up, w_down))
    moe = total.astype(jnp.bfloat16)
    layer_out = (resid + moe.astype(jnp.float32)).astype(jnp.bfloat16)
    return (layer_out, kv_cache)
```

```python
import functools
import math

import jax
import jax.numpy as jnp
from jax import lax
from jax.experimental import pallas as pl
from jax.experimental.pallas import tpu as pltpu
from jax.sharding import PartitionSpec as P

HD = 128
QH = 8
KVH = 2
ROTARY = 1000000.0
NEGATIVE = -1e30
MESH = pl.DeviceIdType.MESH
ANY = pl.BlockSpec(memory_space=pl.ANY)
IN_VMEM = pl.BlockSpec(memory_space=pltpu.VMEM)


def rms_rows(values_in, gain):
    wide = values_in.astype(jnp.float32)
    scale = lax.rsqrt(jnp.mean(wide * wide, axis=-1, keepdims=True) + 1e-06)
    return wide * scale * gain


def rotate(matrix, cosine, sine):
    count = matrix.shape[0]
    shaped = matrix.reshape(count, -1, HD)
    half = HD // 2
    cosine, sine = cosine[:, None, :], sine[:, None, :]
    first = shaped[..., :half]
    second = shaped[..., half:]
    turned = jnp.concatenate(
        [first * cosine - second * sine, second * cosine + first * sine], axis=-1
    )
    return turned.reshape(count, -1)


def greet(peers):
    barrier = pltpu.get_barrier_semaphore()
    for peer in peers:
        pl.semaphore_signal(barrier, inc=1, device_id=peer, device_id_type=MESH)
    pl.semaphore_wait(barrier, len(peers))


def places():
    s, t = lax.axis_index("seq"), lax.axis_index("tp")
    return s, t, s // 16, (s // 2) % 8, s % 2, t // 4, t % 4


def params(number, **more):
    return pltpu.CompilerParams(collective_id=number, has_side_effects=True, **more)


def tp_gather_kernel(
    rows_ref, weight_ref, seg_ref, wide_ref, full_ref, segs_ref,
    send, recv, seg_send, seg_recv, far_send, far_recv, half_send, half_recv, local,
):
    s, t, _, _, core, x, y = places()
    across = (1 - x) * 4
    own = x * 4
    up, down, two = (y + 1) % 4, (y + 3) % 4, (y + 2) % 4
    xp, yn, yp = (s, across + y), (s, own + up), (s, own + down)
    twin = (s + 1 - 2 * core, t)
    tp_peers = [(s, (t + k) % 8) for k in range(1, 8)]
    ahead = [((s + k) % 32, t) for k in range(1, 9)]
    behind = [((s + 32 - k) % 32, t) for k in range(1, 9)]
    greet(tp_peers + ahead + behind + [twin])

    seg_own = pltpu.make_async_copy(seg_ref, segs_ref.at[0, t], local.at[0])
    seg_own.start()
    seg_copies = []
    for k, peer in enumerate(tp_peers):
        copy = pltpu.make_async_remote_copy(
            src_ref=seg_ref, dst_ref=segs_ref.at[0, t], send_sem=seg_send.at[k],
            recv_sem=seg_recv.at[k], device_id=peer, device_id_type=MESH,
        )
        copy.start()
        seg_copies.append(copy)

    sent = []

    def pass_on(bank, number, src, dst, peer):
        copy = pltpu.make_async_remote_copy(
            src_ref=src, dst_ref=dst, send_sem=send.at[bank, number],
            recv_sem=recv.at[bank, number], device_id=peer, device_id_type=MESH,
        )
        copy.start()
        sent.append(copy)

    def landed(bank, number, dst):
        pltpu.make_async_remote_copy(
            src_ref=dst, dst_ref=dst, send_sem=send.at[bank, number],
            recv_sem=recv.at[bank, number], device_id=xp, device_id_type=MESH,
        ).wait_recv()

    banks = [(rows_ref, wide_ref), (weight_ref.at[core], full_ref.at[core])]
    locals_ = []
    for bank, (src, out) in enumerate(banks):
        copy = pltpu.make_async_copy(src, out.at[t], local.at[1 + bank])
        copy.start()
        locals_.append(copy)
        pass_on(bank, 0, src, out.at[t], xp)
        pass_on(bank, 1, src, out.at[t], yn)
        pass_on(bank, 2, src, out.at[t], yp)
    for copy in seg_copies:
        copy.wait()
    seg_own.wait()
    far_copies = []
    for k, peer in enumerate(ahead):
        copy = pltpu.make_async_remote_copy(
            src_ref=segs_ref.at[0], dst_ref=segs_ref.at[k + 1], send_sem=far_send.at[k],
            recv_sem=far_recv.at[k], device_id=peer, device_id_type=MESH,
        )
        copy.start()
        far_copies.append(copy)
    low, high = pl.ds(0, 32), pl.ds(32, 32)
    for bank, (src, out) in enumerate(banks):
        landed(bank, 0, out.at[across + y])
        pass_on(bank, 3, out.at[across + y], out.at[across + y], yn)
        pass_on(bank, 4, out.at[across + y], out.at[across + y], yp)
        landed(bank, 1, out.at[own + down])
        pass_on(bank, 5, out.at[own + down, low], out.at[own + down, low], yn)
        landed(bank, 2, out.at[own + up])
        pass_on(bank, 6, out.at[own + up, high], out.at[own + up, high], yp)
        landed(bank, 3, out.at[across + down])
        pass_on(bank, 7, out.at[across + down, low], out.at[across + down, low], yn)
        landed(bank, 4, out.at[across + up])
        pass_on(bank, 8, out.at[across + up, high], out.at[across + up, high], yp)
    for bank, (src, out) in enumerate(banks):
        landed(bank, 5, out.at[own + two, low])
        landed(bank, 6, out.at[own + two, high])
        landed(bank, 7, out.at[across + two, low])
        landed(bank, 8, out.at[across + two, high])
    for copy in locals_:
        copy.wait()
    halves = pltpu.make_async_remote_copy(
        src_ref=full_ref.at[core], dst_ref=full_ref.at[core], send_sem=half_send,
        recv_sem=half_recv, device_id=twin, device_id_type=MESH,
    )
    halves.start()
    for copy in sent:
        copy.wait_send()
    for copy in far_copies:
        copy.wait()
    halves.wait_send()
    pltpu.make_async_remote_copy(
        src_ref=full_ref.at[1 - core], dst_ref=full_ref.at[1 - core], send_sem=half_send,
        recv_sem=half_recv, device_id=twin, device_id_type=MESH,
    ).wait_recv()


def tp_gather(rows, weight, seg):
    count, width = rows.shape
    dma = pltpu.SemaphoreType.DMA
    return pl.pallas_call(
        tp_gather_kernel,
        out_shape=(
            jax.ShapeDtypeStruct((8, count, width), rows.dtype),
            jax.ShapeDtypeStruct((2, 8, 64, width), weight.dtype),
            jax.ShapeDtypeStruct((9, 8, 1, 128), jnp.int32),
        ),
        in_specs=[ANY] * 3,
        out_specs=(ANY,) * 3,
        scratch_shapes=[
            dma((2, 9)), dma((2, 9)), dma((7,)), dma((7,)), dma((8,)), dma((8,)),
            dma(()), dma(()), dma((3,)),
        ],
        compiler_params=params(1),
        name="tp_gather",
    )(rows, weight, seg)


def kv_kernel(kv_ref, out_ref, z_send, z_recv, y_send, y_recv, c_send, c_recv, local):
    s, t, _, _, core, x, y = places()
    own = x * 4
    up, down, two = (y + 1) % 4, (y + 3) % 4, (y + 2) % 4
    ahead, behind = ((s + 2) % 32, t), ((s + 30) % 32, t)
    yn, yp = (s, own + up), (s, own + down)
    twin = (s + 1 - 2 * core, t)
    greet([ahead, behind, yn, yp, twin])
    first = pltpu.make_async_copy(kv_ref, out_ref.at[0], local)
    first.start()
    sent = []

    def pass_on(src, dst, send_sem, recv_sem, peer):
        copy = pltpu.make_async_remote_copy(
            src_ref=src, dst_ref=dst, send_sem=send_sem, recv_sem=recv_sem,
            device_id=peer, device_id_type=MESH,
        )
        copy.start()
        sent.append(copy)

    def landed(dst, send_sem, recv_sem):
        pltpu.make_async_remote_copy(
            src_ref=dst, dst_ref=dst, send_sem=send_sem, recv_sem=recv_sem,
            device_id=twin, device_id_type=MESH,
        ).wait_recv()

    def to_twin(i):
        pass_on(
            out_ref.at[2 * i + 2 * core], out_ref.at[2 * i + 1],
            c_send.at[i], c_recv.at[i], twin,
        )

    pass_on(kv_ref.at[y], out_ref.at[2, y], z_send.at[0], z_recv.at[0], ahead)
    first.wait()

    def middle(k):
        landed(out_ref.at[2 * k, down], y_send.at[k - 1, 0], y_recv.at[k - 1, 0])
        piece = out_ref.at[2 * k, down, 0]
        pass_on(piece, piece, y_send.at[k - 1, 2], y_recv.at[k - 1, 2], yn)
        landed(out_ref.at[2 * k, up], y_send.at[k - 1, 1], y_recv.at[k - 1, 1])
        piece = out_ref.at[2 * k, up, 1]
        pass_on(piece, piece, y_send.at[k - 1, 3], y_recv.at[k - 1, 3], yp)

    def last(k):
        landed(out_ref.at[2 * k, two, 0], y_send.at[k - 1, 2], y_recv.at[k - 1, 2])
        landed(out_ref.at[2 * k, two, 1], y_send.at[k - 1, 3], y_recv.at[k - 1, 3])

    for k in range(1, 7):
        if k <= 4:
            landed(out_ref.at[2 * k, y], z_send.at[k - 1], z_recv.at[k - 1])
            piece = out_ref.at[2 * k, y]
            if k < 4:
                pass_on(piece, out_ref.at[2 * k + 2, y], z_send.at[k], z_recv.at[k], ahead)
            pass_on(piece, piece, y_send.at[k - 1, 0], y_recv.at[k - 1, 0], yn)
            pass_on(piece, piece, y_send.at[k - 1, 1], y_recv.at[k - 1, 1], yp)
        if 1 <= k - 1 <= 4:
            middle(k - 1)
        if 1 <= k - 2 <= 4:
            last(k - 2)
            to_twin(k - 3)
    for copy in sent:
        copy.wait_send()
    for i in range(4):
        landed(out_ref.at[2 * i + 1], c_send.at[i], c_recv.at[i])


def kv_exchange(kv):
    dma = pltpu.SemaphoreType.DMA
    return pl.pallas_call(
        kv_kernel,
        out_shape=jax.ShapeDtypeStruct((9,) + kv.shape, kv.dtype),
        in_specs=[ANY],
        out_specs=ANY,
        scratch_shapes=[dma((4,)), dma((4,)), dma((4, 4)), dma((4, 4)), dma((4,)), dma((4,)), dma(())],
        compiler_params=params(2),
        name="kv_exchange",
    )(kv)


def attention_kernel(base_ref, q_ref, start_ref, kv_ref, out_ref, peak, total, mixed):
    step = pl.program_id(0)

    @pl.when(step == 0)
    def _():
        peak[...] = jnp.full_like(peak, NEGATIVE)
        total[...] = jnp.zeros_like(total)
        mixed[...] = jnp.zeros_like(mixed)

    count = q_ref.shape[0]
    keys = kv_ref[0, :, 0].reshape(count, HD)
    values = kv_ref[0, :, 1].reshape(count, HD)
    scores = lax.dot_general(
        q_ref[...], keys, (((1,), (1,)), ((), ())), preferred_element_type=jnp.float32
    ) * (1.0 / math.sqrt(HD))
    base = base_ref[0]
    key_index = base - step * count + lax.broadcasted_iota(jnp.int32, (1, count), 1)
    query_index = base + lax.broadcasted_iota(jnp.int32, (count, 1), 0)
    allowed = (key_index >= start_ref[...]) & (key_index <= query_index)
    masked = jnp.where(allowed, scores, NEGATIVE)
    old = peak[...]
    newest = jnp.maximum(old, jnp.max(masked, axis=-1, keepdims=True))
    factor = jnp.exp(old - newest)
    weights = jnp.exp(masked - newest)
    total[...] = total[...] * factor + jnp.sum(weights, axis=-1, keepdims=True)
    mixed[...] = mixed[...] * factor + jnp.dot(
        weights.astype(jnp.bfloat16), values, preferred_element_type=jnp.float32
    )
    peak[...] = newest

    @pl.when(step == pl.num_programs(0) - 1)
    def _():
        out_ref[...] = (mixed[...] / total[...]).astype(out_ref.dtype)


def attend(query, starts, kv_all, base):
    count = query.shape[0]
    whole = lambda shape: pl.BlockSpec(shape, lambda j, _: (0,) * len(shape))
    return pl.pallas_call(
        attention_kernel,
        out_shape=jax.ShapeDtypeStruct((count, HD), jnp.bfloat16),
        grid_spec=pltpu.PrefetchScalarGridSpec(
            num_scalar_prefetch=1,
            grid=(9,),
            in_specs=[
                whole((count, HD)),
                whole((count, 1)),
                pl.BlockSpec((1,) + kv_all.shape[1:], lambda j, _: (j, 0, 0, 0, 0)),
            ],
            out_specs=whole((count, HD)),
            scratch_shapes=[
                pltpu.VMEM((count, 1), jnp.float32),
                pltpu.VMEM((count, 1), jnp.float32),
                pltpu.VMEM((count, HD), jnp.float32),
            ],
        ),
        name="attend",
    )(base, query, starts, kv_all)


def heads_kernel(in_ref, out_ref, send, recv, local):
    s, t, *_ = places()
    peers = [(t + k) % 8 for k in range(1, 8)]
    greet([(s, peer) for peer in peers])
    own = pltpu.make_async_copy(in_ref.at[t], out_ref.at[t], local)
    own.start()
    copies = []
    for k, peer in enumerate(peers):
        copy = pltpu.make_async_remote_copy(
            src_ref=in_ref.at[peer], dst_ref=out_ref.at[t], send_sem=send.at[k],
            recv_sem=recv.at[k], device_id=(s, peer), device_id_type=MESH,
        )
        copy.start()
        copies.append(copy)
    own.wait()
    for copy in copies:
        copy.wait()


def heads_to_tokens(attention):
    dma = pltpu.SemaphoreType.DMA
    return pl.pallas_call(
        heads_kernel,
        out_shape=jax.ShapeDtypeStruct(attention.shape, attention.dtype),
        in_specs=[ANY],
        out_specs=ANY,
        scratch_shapes=[dma((7,)), dma((7,)), dma(())],
        compiler_params=params(3),
        name="heads_to_tokens",
    )(attention)


def spread_kernel(rows_ref, out_ref, x_send, x_recv, z_send, z_recv, c_send, c_recv, local):
    s, t, plane, z, core, x, y = places()
    across = ((1 - plane) * 16 + z * 2 + core, (1 - x) * 4 + y)
    twin = (s + 1 - 2 * core, t)
    ring = [(plane * 16 + ((z + d) % 8) * 2 + core, t) for d in (1, 7)]
    greet([across, twin] + ring)
    planes = [plane, 1 - plane]

    def slot(p, way, distance):
        back = (z + 8 - distance) % 8 if way == 0 else (z + distance) % 8
        return planes[p] * 16 + back * 2 + core

    sent = []

    def pass_on(src, dst, send_sem, recv_sem, peer):
        copy = pltpu.make_async_remote_copy(
            src_ref=src, dst_ref=dst, send_sem=send_sem, recv_sem=recv_sem,
            device_id=peer, device_id_type=MESH,
        )
        copy.start()
        sent.append(copy)

    def landed(dst, send_sem, recv_sem):
        pltpu.make_async_remote_copy(
            src_ref=dst, dst_ref=dst, send_sem=send_sem, recv_sem=recv_sem,
            device_id=twin, device_id_type=MESH,
        ).wait_recv()

    def travels(p, way, distance):
        return distance <= 3 or (distance == 4 and p == way)

    twins = []

    def to_twin(src, block):
        k = len(twins)
        twins.append(k)
        pass_on(src, out_ref.at[block], c_send.at[k], c_recv.at[k], twin)

    own = pltpu.make_async_copy(rows_ref, out_ref.at[s], local)
    own.start()
    pass_on(rows_ref, out_ref.at[s], x_send, x_recv, across)
    for way in range(2):
        pass_on(rows_ref, out_ref.at[s], z_send.at[0, way, 0], z_recv.at[0, way, 0], ring[way])
    to_twin(rows_ref, s)
    block = across[0]
    landed(out_ref.at[block], x_send, x_recv)
    for way in range(2):
        pass_on(out_ref.at[block], out_ref.at[block], z_send.at[1, way, 0], z_recv.at[1, way, 0], ring[way])
    to_twin(out_ref.at[block], block)
    for distance in range(1, 5):
        for p in range(2):
            for way in range(2):
                if not travels(p, way, distance):
                    continue
                block = slot(p, way, distance)
                k = distance - 1
                landed(out_ref.at[block], z_send.at[p, way, k], z_recv.at[p, way, k])
                if travels(p, way, distance + 1):
                    pass_on(
                        out_ref.at[block], out_ref.at[block],
                        z_send.at[p, way, k + 1], z_recv.at[p, way, k + 1], ring[way],
                    )
                to_twin(out_ref.at[block], block)
    own.wait()
    for copy in sent:
        copy.wait_send()
    for k in twins:
        landed(out_ref.at[twin[0]], c_send.at[k], c_recv.at[k])


def spread(rows):
    dma = pltpu.SemaphoreType.DMA
    return pl.pallas_call(
        spread_kernel,
        out_shape=jax.ShapeDtypeStruct((32,) + rows.shape, rows.dtype),
        in_specs=[ANY],
        out_specs=ANY,
        scratch_shapes=[dma(()), dma(()), dma((2, 2, 4)), dma((2, 2, 4)), dma((16,)), dma((16,)), dma(())],
        compiler_params=params(4),
        name="spread",
    )(rows)


CHUNK = 256


def expert_kernel(info_ref, rows_ref, lane_ref, column_ref, gate_ref, up_ref, down_ref, out_ref):
    width = gate_ref.shape[0]
    tokens = rows_ref.shape[0]
    expert, routed = info_ref[0], info_ref[1]

    def one_chunk(number, first):
        base = number * CHUNK
        picks = (
            lane_ref[...] == base + lax.broadcasted_iota(jnp.int32, (CHUNK, 1), 0)
        ).astype(jnp.bfloat16)
        rows = jnp.dot(picks, rows_ref[:, :width], preferred_element_type=jnp.float32).astype(jnp.bfloat16)
        all_gates = jnp.dot(picks, rows_ref[:, width:], preferred_element_type=jnp.float32)
        here = lax.broadcasted_iota(jnp.int32, all_gates.shape, 1) == expert
        gates = jnp.sum(jnp.where(here, all_gates, 0.0), axis=1, keepdims=True)
        gate_out = jnp.dot(rows, gate_ref[...], preferred_element_type=jnp.float32)
        up_out = jnp.dot(rows, up_ref[...], preferred_element_type=jnp.float32)
        active = (jnp.maximum(gate_out, 0.0) * up_out).astype(jnp.bfloat16)
        down_out = jnp.dot(active, down_ref[...], preferred_element_type=jnp.float32) * gates
        contribution = down_out.astype(jnp.bfloat16)
        lanes = base + lax.broadcasted_iota(jnp.int32, (1, CHUNK), 1)

        def place(block, _):
            span = pl.ds(pl.multiple_of(block * CHUNK, CHUNK), CHUNK)
            back = (column_ref[span, :] == lanes).astype(jnp.bfloat16)
            placed = jnp.dot(back, contribution, preferred_element_type=jnp.float32)
            if not first:
                placed = placed + out_ref[span, :].astype(jnp.float32)
            out_ref[span, :] = placed.astype(jnp.bfloat16)
            return 0

        lax.fori_loop(0, tokens // CHUNK, place, 0)

    one_chunk(0, True)

    def more(number, _):
        one_chunk(number, False)
        return 0

    lax.fori_loop(1, (routed + CHUNK - 1) // CHUNK, more, 0)


def run_expert(info, rows, lane_slots, column_slots, w_gate, w_up, w_down):
    tokens = rows.shape[0]
    return pl.pallas_call(
        expert_kernel,
        out_shape=jax.ShapeDtypeStruct((tokens, w_gate.shape[0]), jnp.bfloat16),
        in_specs=[pl.BlockSpec(memory_space=pltpu.SMEM)] + [IN_VMEM] * 6,
        out_specs=IN_VMEM,
        compiler_params=pltpu.CompilerParams(vmem_limit_bytes=60 << 20),
        name="run_expert",
    )(info, rows, lane_slots, column_slots, w_gate, w_up, w_down)


def collect_kernel(
    in_ref, out_ref, mine, other, ring_in, final, from_x,
    x_send, x_recv, z_send, z_recv, c_send, c_recv, local,
):
    s, t, plane, z, core, x, y = places()
    across = ((1 - plane) * 16 + z * 2 + core, (1 - x) * 4 + y)
    twin = (s + 1 - 2 * core, t)
    ring = [(plane * 16 + ((z + d) % 8) * 2 + core, t) for d in (1, 7)]
    greet([across, twin] + ring)
    planes = [plane, 1 - plane]

    def place(p, way, distance):
        ahead = (z + distance) % 8 if way == 0 else (z + 8 - distance) % 8
        return planes[p] * 8 + ahead

    order = [(0, 0, 4), (1, 1, 4)]
    for distance in (3, 2, 1):
        for p in range(2):
            for way in range(2):
                order.append((p, way, distance))
    order += [(1, 0, 0), (0, 0, 0)]
    loads, swaps = [], []
    for k, key in enumerate(order):
        i = place(*key)
        swap = pltpu.make_async_remote_copy(
            src_ref=in_ref.at[2 * i + 1 - core], dst_ref=other.at[i], send_sem=c_send.at[k],
            recv_sem=c_recv.at[k], device_id=twin, device_id_type=MESH,
        )
        swap.start()
        swaps.append(swap)
        load = pltpu.make_async_copy(in_ref.at[2 * i + core], mine.at[i], local.at[k])
        load.start()
        loads.append(load)

    sent = []

    def pass_on(src, dst, send_sem, recv_sem, peer):
        copy = pltpu.make_async_remote_copy(
            src_ref=src, dst_ref=dst, send_sem=send_sem, recv_sem=recv_sem,
            device_id=peer, device_id_type=MESH,
        )
        copy.start()
        sent.append(copy)

    def landed(dst, send_sem, recv_sem):
        pltpu.make_async_remote_copy(
            src_ref=dst, dst_ref=dst, send_sem=send_sem, recv_sem=recv_sem,
            device_id=twin, device_id_type=MESH,
        ).wait_recv()

    wide = lambda ref: ref[...].astype(jnp.float32)
    for k, (p, way, distance) in enumerate(order):
        i = place(p, way, distance)
        loads[k].wait()
        swaps[k].wait()
        if distance == 0:
            break
        total = wide(mine.at[i]) + wide(other.at[i])
        farther = 3 if p != way else 4
        if distance < farther:
            piece = ring_in.at[p, way, distance]
            landed(piece, z_send.at[p, way, distance], z_recv.at[p, way, distance])
            total = total + wide(piece)
        mine[i] = total.astype(jnp.bfloat16)
        pass_on(
            mine.at[i], ring_in.at[p, way, distance - 1],
            z_send.at[p, way, distance - 1], z_recv.at[p, way, distance - 1], ring[way],
        )
    loads[-1].wait()
    swaps[-1].wait()
    for p in (1, 0):
        i = planes[p] * 8 + z
        total = wide(mine.at[i]) + wide(other.at[i])
        for way in range(2):
            piece = ring_in.at[p, way, 0]
            landed(piece, z_send.at[p, way, 0], z_recv.at[p, way, 0])
            total = total + wide(piece)
        if p == 1:
            final[...] = total.astype(jnp.bfloat16)
            pass_on(final, from_x, x_send, x_recv, across)
        else:
            landed(from_x, x_send, x_recv)
            out_ref[...] = (total + wide(from_x)).astype(out_ref.dtype)
    for copy in sent:
        copy.wait_send()


def collect(parts):
    dma = pltpu.SemaphoreType.DMA
    rows = parts.shape[1:]
    vmem = lambda *lead: pltpu.VMEM(lead + rows, parts.dtype)
    return pl.pallas_call(
        collect_kernel,
        out_shape=jax.ShapeDtypeStruct(rows, jnp.bfloat16),
        in_specs=[ANY],
        out_specs=IN_VMEM,
        scratch_shapes=[
            vmem(16), vmem(16), vmem(2, 2, 4), vmem(), vmem(),
            dma(()), dma(()), dma((2, 2, 4)), dma((2, 2, 4)), dma((16,)), dma((16,)), dma((16,)),
        ],
        compiler_params=params(5, vmem_limit_bytes=40 << 20),
        name="collect",
    )(parts)


def on_device(
    tokens, segment_ids, routes, attn_gain, w_query, w_key, w_value, w_out,
    moe_gain, w_router, w_gate, w_up, w_down,
):
    tp_rank = lax.axis_index("tp")
    seq_rank = lax.axis_index("seq")
    tok_dev, width = tokens.shape
    tok_seq = tok_dev * 8
    bf16, f32 = jnp.bfloat16, jnp.float32
    block_first = seq_rank * tok_seq

    seg_row = jnp.pad(segment_ids, (0, HD - tok_dev), constant_values=-1).reshape(1, HD)
    wide, w_out_all, segs = tp_gather(tokens, w_out.reshape(2, HD // 2, width), seg_row)

    block_index = block_first + jnp.arange(tok_seq, dtype=jnp.int32)
    near = segs[:, :, 0, :tok_dev].reshape(9, tok_seq)
    near_index = block_index[None, :] - tok_seq * jnp.arange(9, dtype=jnp.int32)[:, None]
    labels = jnp.arange(6, dtype=jnp.int32)
    hits = (near[None] == labels[:, None, None]) & (near_index >= 0)[None]
    firsts = jnp.min(jnp.where(hits, near_index[None], 1 << 30), axis=(1, 2))
    starts = jnp.sum(jnp.where(near[0][:, None] == labels[None, :], firsts[None, :], 0), axis=1)
    position = (block_index - starts).astype(f32)
    inverse = ROTARY ** (-(jnp.arange(HD // 2, dtype=f32) * 2.0 / HD))
    angle = position[:, None] * inverse[None, :]
    cosine, sine = jnp.cos(angle), jnp.sin(angle)

    normed = rms_rows(wide.reshape(tok_seq, width), attn_gain).astype(bf16)
    query = rotate(jnp.dot(normed, w_query, preferred_element_type=f32), cosine, sine).astype(bf16)
    keys = rotate(jnp.dot(normed, w_key, preferred_element_type=f32), cosine, sine).astype(bf16)
    values = jnp.dot(normed, w_value, preferred_element_type=f32).astype(bf16)

    def own_rows(matrix):
        mine = lax.dynamic_slice_in_dim(matrix, tp_rank * tok_dev, tok_dev, 0)
        return jnp.transpose(mine.reshape(tok_dev, KVH, HD), (1, 0, 2))

    kv_cache = jnp.stack([own_rows(keys), own_rows(values)])
    head = tp_rank // 4
    kv_own = jnp.stack(
        [
            lax.dynamic_slice_in_dim(m, head * HD, HD, 1).reshape(4, tok_seq // 4, HD)
            for m in (keys, values)
        ],
        axis=1,
    )
    kv_all = kv_exchange(kv_own)
    attention = attend(query, starts[:, None], kv_all, block_first[None])
    by_head = heads_to_tokens(attention.reshape(8, tok_dev, HD))
    split = jnp.transpose(by_head.reshape(8, tok_dev, 2, HD // 2), (1, 2, 0, 3))
    resid = tokens.astype(f32) + jnp.dot(
        split.reshape(tok_dev, QH * HD), w_out_all.reshape(QH * HD, width), preferred_element_type=f32
    )
    moe_rows = rms_rows(resid, moe_gain).astype(bf16)
    experts = w_router.shape[1]
    logits = jnp.dot(moe_rows, w_router, preferred_element_type=f32)
    expert_ids = jnp.arange(experts, dtype=jnp.int32)
    chosen_one = routes[:, :, None] == expert_ids[None, None, :]
    chosen = jnp.sum(jnp.where(chosen_one, logits[:, None, :], 0.0), axis=-1)
    gates = jax.nn.softmax(chosen, axis=-1).astype(bf16)
    gate_table = jnp.sum(jnp.where(chosen_one, gates[:, :, None], 0), axis=1).astype(bf16)
    payload = jnp.concatenate([moe_rows, jnp.pad(gate_table, ((0, 0), (0, HD - experts)))], axis=1)

    arrived = spread(payload).reshape(32 * tok_dev, width + HD)
    my_gates = lax.dynamic_slice_in_dim(arrived[:, width:], seq_rank, 1, 1)[:, 0]
    routed = (my_gates != 0).reshape(16, HD)
    ones = routed.astype(bf16)
    upto = jnp.arange(HD)[:, None] <= jnp.arange(HD)[None, :]
    inside = jnp.dot(ones, upto.astype(bf16), preferred_element_type=f32)
    sums = inside[:, -1]
    before = jnp.sum(jnp.where(jnp.arange(16)[None, :] < jnp.arange(16)[:, None], sums[None, :], 0.0), axis=1)
    slots = jnp.where(routed, (inside + before[:, None]).astype(jnp.int32) - 1, -1)
    total = jnp.sum(sums).astype(jnp.int32)
    info = jnp.stack([seq_rank.astype(jnp.int32), total])
    parts = run_expert(
        info, arrived, slots.reshape(1, -1), slots.reshape(-1, 1), w_gate[0], w_up[0], w_down[0]
    )
    moe = collect(parts.reshape(32, tok_dev, width))
    layer_out = (resid + moe.astype(f32)).astype(bf16)
    return (layer_out, kv_cache)


def solution(mesh):
    placed = (
        P(("seq", "tp"), None),
        P(("seq", "tp")),
        P(("seq", "tp"), None),
        P(),
        P(None, "tp"),
        P(),
        P(),
        P("tp", None),
        P(),
        P(),
        P("seq", None, None),
        P("seq", None, None),
        P("seq", None, None),
    )
    return jax.shard_map(
        on_device,
        mesh=mesh,
        in_specs=placed,
        out_specs=(P(("seq", "tp"), None), P(None, None, ("seq", "tp"), None)),
        check_vma=False,
    )
```

```python
import functools
import math

import jax
import jax.numpy as jnp
from jax import lax
from jax.experimental import pallas as pl
from jax.experimental.pallas import tpu as pltpu
from jax.sharding import PartitionSpec as P

HD = 128
QH = 8
KVH = 2
ROTARY = 1000000.0
NEGATIVE = -1e30
MESH = pl.DeviceIdType.MESH
ANY = pl.BlockSpec(memory_space=pl.ANY)
IN_VMEM = pl.BlockSpec(memory_space=pltpu.VMEM)


def rms_rows(values_in, gain):
    wide = values_in.astype(jnp.float32)
    scale = lax.rsqrt(jnp.mean(wide * wide, axis=-1, keepdims=True) + 1e-06)
    return wide * scale * gain


def rotate(matrix, cosine, sine):
    count = matrix.shape[0]
    shaped = matrix.reshape(count, -1, HD)
    half = HD // 2
    cosine, sine = cosine[:, None, :], sine[:, None, :]
    first = shaped[..., :half]
    second = shaped[..., half:]
    turned = jnp.concatenate(
        [first * cosine - second * sine, second * cosine + first * sine], axis=-1
    )
    return turned.reshape(count, -1)


def greet(peers):
    barrier = pltpu.get_barrier_semaphore()
    for peer in peers:
        pl.semaphore_signal(barrier, inc=1, device_id=peer, device_id_type=MESH)
    pl.semaphore_wait(barrier, len(peers))


def places():
    s, t = lax.axis_index("seq"), lax.axis_index("tp")
    return s, t, s // 16, (s // 2) % 8, s % 2, t // 4, t % 4


def params(number, **more):
    return pltpu.CompilerParams(collective_id=number, has_side_effects=True, **more)


class Copies:
    def __init__(self, anyone):
        self.anyone, self.sent = anyone, []

    def start(self, src, dst, send, recv, peer):
        copy = pltpu.make_async_remote_copy(
            src_ref=src, dst_ref=dst, send_sem=send, recv_sem=recv,
            device_id=peer, device_id_type=MESH,
        )
        copy.start()
        self.sent.append(copy)

    def landed(self, dst, send, recv):
        pltpu.make_async_remote_copy(
            src_ref=dst, dst_ref=dst, send_sem=send, recv_sem=recv,
            device_id=self.anyone, device_id_type=MESH,
        ).wait_recv()

    def drain(self):
        for copy in self.sent:
            copy.wait_send()


def tp_gather_kernel(
    rows_ref, seg_ref, out, segs_ref,
    send, recv, seg_send, seg_recv, far_send, far_recv, local,
):
    s, t, _, _, core, x, y = places()
    across = (1 - x) * 4
    own = x * 4
    up, down, two = (y + 1) % 4, (y + 3) % 4, (y + 2) % 4
    xp, yn, yp = (s, across + y), (s, own + up), (s, own + down)
    tp_peers = [(s, (t + k) % 8) for k in range(1, 8)]
    ahead = [((s + k) % 32, t) for k in range(1, 9)]
    behind = [((s + 32 - k) % 32, t) for k in range(1, 9)]
    greet(tp_peers + ahead + behind)
    moves = Copies(xp)

    def go(number, src, dst, peer):
        moves.start(src, dst, send.at[number], recv.at[number], peer)

    def landed(number, dst):
        moves.landed(dst, send.at[number], recv.at[number])

    seg_own = pltpu.make_async_copy(seg_ref, segs_ref.at[0, t], local.at[0])
    seg_own.start()
    for k, peer in enumerate(tp_peers):
        moves.start(seg_ref, segs_ref.at[0, t], seg_send.at[k], seg_recv.at[k], peer)
    go(0, rows_ref, out.at[t], xp)
    go(1, rows_ref, out.at[t], yn)
    go(2, rows_ref, out.at[t], yp)
    rows_own = pltpu.make_async_copy(rows_ref, out.at[t], local.at[1])
    rows_own.start()
    seg_own.wait()
    for k in range(7):
        moves.landed(segs_ref.at[0, t], seg_send.at[k], seg_recv.at[k])
    for k, peer in enumerate(ahead):
        moves.start(segs_ref.at[0], segs_ref.at[k + 1], far_send.at[k], far_recv.at[k], peer)
    low, high = pl.ds(0, 32), pl.ds(32, 32)
    landed(0, out.at[across + y])
    go(3, out.at[across + y], out.at[across + y], yn)
    go(4, out.at[across + y], out.at[across + y], yp)
    landed(1, out.at[own + down])
    go(5, out.at[own + down, low], out.at[own + down, low], yn)
    landed(2, out.at[own + up])
    go(6, out.at[own + up, high], out.at[own + up, high], yp)
    landed(3, out.at[across + down])
    go(7, out.at[across + down, low], out.at[across + down, low], yn)
    landed(4, out.at[across + up])
    go(8, out.at[across + up, high], out.at[across + up, high], yp)
    landed(5, out.at[own + two, low])
    landed(6, out.at[own + two, high])
    landed(7, out.at[across + two, low])
    landed(8, out.at[across + two, high])
    rows_own.wait()
    for k in range(8):
        moves.landed(segs_ref.at[k + 1], far_send.at[k], far_recv.at[k])
    moves.drain()


def tp_gather(rows, seg):
    count, width = rows.shape
    dma = pltpu.SemaphoreType.DMA
    return pl.pallas_call(
        tp_gather_kernel,
        out_shape=(
            jax.ShapeDtypeStruct((8, count, width), rows.dtype),
            jax.ShapeDtypeStruct((9, 8, 1, 128), jnp.int32),
        ),
        in_specs=[IN_VMEM] * 2,
        out_specs=(IN_VMEM,) * 2,
        scratch_shapes=[dma((9,)), dma((9,)), dma((7,)), dma((7,)), dma((8,)), dma((8,)), dma((2,))],
        compiler_params=params(1, vmem_limit_bytes=16 << 20),
        name="tp_gather",
    )(rows, seg)


TILE = 128


def attention_kernel(
    kv_ref, q_ref, start_ref, tokens_ref, w_out_ref, gain_ref, router_ref, routes_ref,
    resid_ref, payload_ref,
    slots, w_full, peak, total, mixed, heads_out, heads_in,
    z_send, z_recv, y_send, y_recv, c_send, c_recv,
    w_send, w_recv, t_send, t_recv, h_send, h_recv, local,
):
    s, t, _, _, core, x, y = places()
    across, own = (1 - x) * 4, x * 4
    up, down, two = (y + 1) % 4, (y + 3) % 4, (y + 2) % 4
    far = ((s + 4) % 32, t)
    near = ((s + 2) % 32, t)
    xp, yn, yp = (s, across + y), (s, own + up), (s, own + down)
    twin = (s + 1 - 2 * core, t)
    tp_peers = [(s, (t + k) % 8) for k in range(1, 8)]
    greet(tp_peers + [twin, near, far, ((s + 30) % 32, t), ((s + 28) % 32, t)])
    moves = Copies(twin)
    count = q_ref.shape[0]

    def w_piece(rank, half, first=0, rows=64):
        return w_full.at[rank, pl.ds(pl.multiple_of(half * 64 + first, 32), rows)]

    def w_go(number, rank, peer, first=0, rows=64):
        piece = w_piece(rank, core, first, rows)
        moves.start(piece, piece, w_send.at[number], w_recv.at[number], peer)

    def w_landed(number, rank, first=0, rows=64):
        moves.landed(w_piece(rank, core, first, rows), w_send.at[number], w_recv.at[number])

    def w_twin(number, rank):
        piece = w_piece(rank, core)
        moves.start(piece, piece, t_send.at[number], t_recv.at[number], twin)

    kv_own = pltpu.make_async_copy(kv_ref, slots.at[0], local.at[0])
    kv_own.start()
    w_own = pltpu.make_async_copy(w_out_ref, w_full.at[t], local.at[1])
    w_own.start()
    moves.start(kv_ref.at[y], slots.at[2, y], z_send.at[0], z_recv.at[0], near)
    moves.start(kv_ref.at[y], slots.at[4, y], z_send.at[1], z_recv.at[1], far)
    w_own.wait()
    w_go(0, t, xp)
    w_go(1, t, yn)
    w_go(2, t, yp)

    peak[...] = jnp.full_like(peak, NEGATIVE)
    total[...] = jnp.zeros_like(total)
    mixed[...] = jnp.zeros_like(mixed)
    base = s * count
    unit = math.log2(math.e) / math.sqrt(HD)

    def attend(j):
        def tile(number, _):
            rows = pl.ds(pl.multiple_of(number * TILE, TILE), TILE)
            keys = slots[j, :, 0].reshape(count, HD)
            values = slots[j, :, 1].reshape(count, HD)
            scores = lax.dot_general(
                q_ref[rows, :], keys, (((1,), (1,)), ((), ())), preferred_element_type=jnp.float32
            ) * unit
            key_index = base - j * count + lax.broadcasted_iota(jnp.int32, (1, count), 1)
            allowed = key_index >= start_ref[rows, :]
            if j == 0:
                query_index = base + number * TILE + lax.broadcasted_iota(jnp.int32, (TILE, 1), 0)
                allowed = allowed & (key_index <= query_index)
            masked = jnp.where(allowed, scores, NEGATIVE)
            old = peak[rows, :]
            newest = jnp.maximum(old, jnp.max(masked, axis=-1, keepdims=True))
            factor = jnp.exp2(old - newest)
            weights = jnp.exp2(masked - newest)
            total[rows, :] = total[rows, :] * factor + jnp.sum(weights, axis=-1, keepdims=True)
            mixed[rows, :] = mixed[rows, :] * factor + jnp.dot(
                weights.astype(jnp.bfloat16), values, preferred_element_type=jnp.float32
            )
            peak[rows, :] = newest
            return 0

        lax.fori_loop(0, count // TILE, tile, 0)

    def z_step(k, onward):
        piece = slots.at[2 * k, y]
        moves.landed(piece, z_send.at[k - 1], z_recv.at[k - 1])
        if onward:
            moves.start(piece, slots.at[2 * k + 4, y], z_send.at[k + 1], z_recv.at[k + 1], far)
        moves.start(piece, piece, y_send.at[k - 1, 0], y_recv.at[k - 1, 0], yn)
        moves.start(piece, piece, y_send.at[k - 1, 1], y_recv.at[k - 1, 1], yp)

    def y_step(k):
        moves.landed(slots.at[2 * k, down], y_send.at[k - 1, 0], y_recv.at[k - 1, 0])
        piece = slots.at[2 * k, down, 0]
        moves.start(piece, piece, y_send.at[k - 1, 2], y_recv.at[k - 1, 2], yn)
        moves.landed(slots.at[2 * k, up], y_send.at[k - 1, 1], y_recv.at[k - 1, 1])
        piece = slots.at[2 * k, up, 1]
        moves.start(piece, piece, y_send.at[k - 1, 3], y_recv.at[k - 1, 3], yp)

    def block_step(k):
        moves.landed(slots.at[2 * k, two, 0], y_send.at[k - 1, 2], y_recv.at[k - 1, 2])
        moves.landed(slots.at[2 * k, two, 1], y_send.at[k - 1, 3], y_recv.at[k - 1, 3])
        moves.start(
            slots.at[2 * k - 2 + 2 * core], slots.at[2 * k - 1], c_send.at[k - 1], c_recv.at[k - 1], twin
        )

    def twin_step(k):
        moves.landed(slots.at[2 * k - 1], c_send.at[k - 1], c_recv.at[k - 1])
        attend(2 * k - 1)

    kv_own.wait()
    attend(0)
    z_step(1, True)
    z_step(2, True)
    w_landed(0, across + y)
    w_go(3, across + y, yn)
    w_go(4, across + y, yp)
    w_twin(0, across + y)
    y_step(1)
    y_step(2)
    w_landed(1, own + down)
    w_go(5, own + down, yn, 0, 32)
    w_twin(1, own + down)
    w_landed(2, own + up)
    w_go(6, own + up, yp, 32, 32)
    w_twin(2, own + up)
    block_step(1)
    attend(2)
    z_step(3, False)
    z_step(4, False)
    block_step(2)
    twin_step(1)
    y_step(3)
    y_step(4)
    attend(4)
    w_landed(3, across + down)
    w_go(7, across + down, yn, 0, 32)
    w_twin(3, across + down)
    w_landed(4, across + up)
    w_go(8, across + up, yp, 32, 32)
    w_twin(4, across + up)
    block_step(3)
    twin_step(2)
    block_step(4)
    attend(6)
    twin_step(3)
    w_landed(5, own + two, 0, 32)
    w_landed(6, own + two, 32, 32)
    w_twin(5, own + two)
    attend(8)
    w_landed(7, across + two, 0, 32)
    w_landed(8, across + two, 32, 32)
    w_twin(6, across + two)
    twin_step(4)

    for rank in range(8):
        rows = pl.ds(rank * 64, 64)
        heads_out[rank] = (mixed[rows, :] / total[rows, :]).astype(heads_out.dtype)
    heads_own = pltpu.make_async_copy(heads_out.at[t], heads_in.at[t], local.at[0])
    heads_own.start()
    for k, peer in enumerate(tp_peers):
        moves.start(heads_out.at[peer[1]], heads_in.at[t], h_send.at[k], h_recv.at[k], peer)
    ranks = [across + y, own + down, own + up, across + down, across + up, own + two, across + two]
    for number, rank in enumerate(ranks):
        moves.landed(w_piece(rank, 1 - core), t_send.at[number], t_recv.at[number])
    heads_own.wait()
    for k in range(7):
        moves.landed(heads_in.at[t], h_send.at[k], h_recv.at[k])
    attention = jnp.concatenate([heads_in[rank] for rank in range(8)], axis=1)
    width = tokens_ref.shape[1]
    resid = tokens_ref[...].astype(jnp.float32) + jnp.dot(
        attention, w_full[...].reshape(8 * HD, width), preferred_element_type=jnp.float32
    )
    resid_ref[...] = resid
    moe_rows = rms_rows(resid, gain_ref[...]).astype(jnp.bfloat16)
    payload_ref[:, :width] = moe_rows
    logits = jnp.dot(moe_rows, router_ref[...], preferred_element_type=jnp.float32)
    experts = logits.shape[1]
    expert_ids = lax.broadcasted_iota(jnp.int32, logits.shape, 1)
    routes = routes_ref[...]
    picked = [routes[:, k : k + 1] == expert_ids for k in range(routes.shape[1])]
    chosen = [jnp.sum(jnp.where(one, logits, 0.0), axis=1, keepdims=True) for one in picked]
    highest = functools.reduce(jnp.maximum, chosen)
    powers = [jnp.exp(one - highest) for one in chosen]
    whole = functools.reduce(jnp.add, powers)
    table = jnp.zeros_like(logits)
    for one, power in zip(picked, powers):
        table = jnp.where(one, power / whole, table)
    payload_ref[:, width:] = jnp.zeros((logits.shape[0], HD), jnp.bfloat16)
    payload_ref[:, width : width + experts] = table.astype(jnp.bfloat16)
    moves.drain()


def attention_layer(kv, query, starts, tokens, w_out, gain, router, routes):
    dma = pltpu.SemaphoreType.DMA
    bf16, f32 = jnp.bfloat16, jnp.float32
    rows, width = tokens.shape
    count = query.shape[0]
    return pl.pallas_call(
        attention_kernel,
        out_shape=(
            jax.ShapeDtypeStruct((rows, width), f32),
            jax.ShapeDtypeStruct((rows, width + HD), bf16),
        ),
        in_specs=[IN_VMEM] * 8,
        out_specs=(IN_VMEM,) * 2,
        scratch_shapes=[
            pltpu.VMEM((9,) + kv.shape, bf16),
            pltpu.VMEM((8, HD, width), bf16),
            pltpu.VMEM((count, 1), f32),
            pltpu.VMEM((count, 1), f32),
            pltpu.VMEM((count, HD), f32),
            pltpu.VMEM((8, rows, HD), bf16),
            pltpu.VMEM((8, rows, HD), bf16),
            dma((4,)), dma((4,)), dma((4, 4)), dma((4, 4)), dma((4,)), dma((4,)),
            dma((9,)), dma((9,)), dma((7,)), dma((7,)), dma((7,)), dma((7,)), dma((2,)),
        ],
        compiler_params=params(2, vmem_limit_bytes=32 << 20),
        name="attention_layer",
    )(kv, query, starts, tokens, w_out, gain, router, routes)


def spread_kernel(rows_ref, out_ref, x_send, x_recv, z_send, z_recv, c_send, c_recv, local):
    s, t, plane, z, core, x, y = places()
    across = ((1 - plane) * 16 + z * 2 + core, (1 - x) * 4 + y)
    twin = (s + 1 - 2 * core, t)
    ring = [(plane * 16 + ((z + d) % 8) * 2 + core, t) for d in (1, 7)]
    greet([across, twin] + ring)
    planes = [plane, 1 - plane]

    def slot(p, way, distance):
        back = (z + 8 - distance) % 8 if way == 0 else (z + distance) % 8
        return planes[p] * 16 + back * 2 + core

    sent = []

    def pass_on(src, dst, send_sem, recv_sem, peer):
        copy = pltpu.make_async_remote_copy(
            src_ref=src, dst_ref=dst, send_sem=send_sem, recv_sem=recv_sem,
            device_id=peer, device_id_type=MESH,
        )
        copy.start()
        sent.append(copy)

    def landed(dst, send_sem, recv_sem):
        pltpu.make_async_remote_copy(
            src_ref=dst, dst_ref=dst, send_sem=send_sem, recv_sem=recv_sem,
            device_id=twin, device_id_type=MESH,
        ).wait_recv()

    def travels(p, way, distance):
        return distance <= 3 or (distance == 4 and p == way)

    twins = []

    def to_twin(src, block):
        k = len(twins)
        twins.append(k)
        pass_on(src, out_ref.at[block], c_send.at[k], c_recv.at[k], twin)

    own = pltpu.make_async_copy(rows_ref, out_ref.at[s], local)
    own.start()
    pass_on(rows_ref, out_ref.at[s], x_send, x_recv, across)
    for way in range(2):
        pass_on(rows_ref, out_ref.at[s], z_send.at[0, way, 0], z_recv.at[0, way, 0], ring[way])
    to_twin(rows_ref, s)
    block = across[0]
    landed(out_ref.at[block], x_send, x_recv)
    for way in range(2):
        pass_on(out_ref.at[block], out_ref.at[block], z_send.at[1, way, 0], z_recv.at[1, way, 0], ring[way])
    to_twin(out_ref.at[block], block)
    for distance in range(1, 5):
        for p in range(2):
            for way in range(2):
                if not travels(p, way, distance):
                    continue
                block = slot(p, way, distance)
                k = distance - 1
                landed(out_ref.at[block], z_send.at[p, way, k], z_recv.at[p, way, k])
                if travels(p, way, distance + 1):
                    pass_on(
                        out_ref.at[block], out_ref.at[block],
                        z_send.at[p, way, k + 1], z_recv.at[p, way, k + 1], ring[way],
                    )
                to_twin(out_ref.at[block], block)
    own.wait()
    for copy in sent:
        copy.wait_send()
    for k in twins:
        landed(out_ref.at[twin[0]], c_send.at[k], c_recv.at[k])


def spread(rows):
    dma = pltpu.SemaphoreType.DMA
    return pl.pallas_call(
        spread_kernel,
        out_shape=jax.ShapeDtypeStruct((32,) + rows.shape, rows.dtype),
        in_specs=[ANY],
        out_specs=ANY,
        scratch_shapes=[dma(()), dma(()), dma((2, 2, 4)), dma((2, 2, 4)), dma((16,)), dma((16,)), dma(())],
        compiler_params=params(4),
        name="spread",
    )(rows)


CHUNK = 256


def expert_kernel(info_ref, rows_ref, lane_ref, column_ref, gate_ref, up_ref, down_ref, out_ref):
    width = gate_ref.shape[0]
    tokens = rows_ref.shape[0]
    expert, routed = info_ref[0], info_ref[1]

    def one_chunk(number, first):
        base = number * CHUNK
        picks = (
            lane_ref[...] == base + lax.broadcasted_iota(jnp.int32, (CHUNK, 1), 0)
        ).astype(jnp.bfloat16)
        rows = jnp.dot(picks, rows_ref[:, :width], preferred_element_type=jnp.float32).astype(jnp.bfloat16)
        all_gates = jnp.dot(picks, rows_ref[:, width:], preferred_element_type=jnp.float32)
        here = lax.broadcasted_iota(jnp.int32, all_gates.shape, 1) == expert
        gates = jnp.sum(jnp.where(here, all_gates, 0.0), axis=1, keepdims=True)
        gate_out = jnp.dot(rows, gate_ref[...], preferred_element_type=jnp.float32)
        up_out = jnp.dot(rows, up_ref[...], preferred_element_type=jnp.float32)
        active = (jnp.maximum(gate_out, 0.0) * up_out).astype(jnp.bfloat16)
        down_out = jnp.dot(active, down_ref[...], preferred_element_type=jnp.float32) * gates
        contribution = down_out.astype(jnp.bfloat16)
        lanes = base + lax.broadcasted_iota(jnp.int32, (1, CHUNK), 1)

        def place(block, _):
            span = pl.ds(pl.multiple_of(block * CHUNK, CHUNK), CHUNK)
            back = (column_ref[span, :] == lanes).astype(jnp.bfloat16)
            placed = jnp.dot(back, contribution, preferred_element_type=jnp.float32)
            if not first:
                placed = placed + out_ref[span, :].astype(jnp.float32)
            out_ref[span, :] = placed.astype(jnp.bfloat16)
            return 0

        lax.fori_loop(0, tokens // CHUNK, place, 0)

    one_chunk(0, True)

    def more(number, _):
        one_chunk(number, False)
        return 0

    lax.fori_loop(1, (routed + CHUNK - 1) // CHUNK, more, 0)


def run_expert(info, rows, lane_slots, column_slots, w_gate, w_up, w_down):
    tokens = rows.shape[0]
    return pl.pallas_call(
        expert_kernel,
        out_shape=jax.ShapeDtypeStruct((tokens, w_gate.shape[0]), jnp.bfloat16),
        in_specs=[pl.BlockSpec(memory_space=pltpu.SMEM)] + [IN_VMEM] * 6,
        out_specs=IN_VMEM,
        compiler_params=pltpu.CompilerParams(vmem_limit_bytes=60 << 20),
        name="run_expert",
    )(info, rows, lane_slots, column_slots, w_gate, w_up, w_down)


def collect_kernel(
    in_ref, out_ref, mine, other, ring_in, final, from_x,
    x_send, x_recv, z_send, z_recv, c_send, c_recv, local,
):
    s, t, plane, z, core, x, y = places()
    across = ((1 - plane) * 16 + z * 2 + core, (1 - x) * 4 + y)
    twin = (s + 1 - 2 * core, t)
    ring = [(plane * 16 + ((z + d) % 8) * 2 + core, t) for d in (1, 7)]
    greet([across, twin] + ring)
    planes = [plane, 1 - plane]

    def place(p, way, distance):
        ahead = (z + distance) % 8 if way == 0 else (z + 8 - distance) % 8
        return planes[p] * 8 + ahead

    order = [(0, 0, 4), (1, 1, 4)]
    for distance in (3, 2, 1):
        for p in range(2):
            for way in range(2):
                order.append((p, way, distance))
    order += [(1, 0, 0), (0, 0, 0)]
    loads, swaps = [], []
    for k, key in enumerate(order):
        i = place(*key)
        swap = pltpu.make_async_remote_copy(
            src_ref=in_ref.at[2 * i + 1 - core], dst_ref=other.at[i], send_sem=c_send.at[k],
            recv_sem=c_recv.at[k], device_id=twin, device_id_type=MESH,
        )
        swap.start()
        swaps.append(swap)
        load = pltpu.make_async_copy(in_ref.at[2 * i + core], mine.at[i], local.at[k])
        load.start()
        loads.append(load)

    sent = []

    def pass_on(src, dst, send_sem, recv_sem, peer):
        copy = pltpu.make_async_remote_copy(
            src_ref=src, dst_ref=dst, send_sem=send_sem, recv_sem=recv_sem,
            device_id=peer, device_id_type=MESH,
        )
        copy.start()
        sent.append(copy)

    def landed(dst, send_sem, recv_sem):
        pltpu.make_async_remote_copy(
            src_ref=dst, dst_ref=dst, send_sem=send_sem, recv_sem=recv_sem,
            device_id=twin, device_id_type=MESH,
        ).wait_recv()

    wide = lambda ref: ref[...].astype(jnp.float32)
    for k, (p, way, distance) in enumerate(order):
        i = place(p, way, distance)
        loads[k].wait()
        swaps[k].wait()
        if distance == 0:
            break
        total = wide(mine.at[i]) + wide(other.at[i])
        farther = 3 if p != way else 4
        if distance < farther:
            piece = ring_in.at[p, way, distance]
            landed(piece, z_send.at[p, way, distance], z_recv.at[p, way, distance])
            total = total + wide(piece)
        mine[i] = total.astype(jnp.bfloat16)
        pass_on(
            mine.at[i], ring_in.at[p, way, distance - 1],
            z_send.at[p, way, distance - 1], z_recv.at[p, way, distance - 1], ring[way],
        )
    loads[-1].wait()
    swaps[-1].wait()
    for p in (1, 0):
        i = planes[p] * 8 + z
        total = wide(mine.at[i]) + wide(other.at[i])
        for way in range(2):
            piece = ring_in.at[p, way, 0]
            landed(piece, z_send.at[p, way, 0], z_recv.at[p, way, 0])
            total = total + wide(piece)
        if p == 1:
            final[...] = total.astype(jnp.bfloat16)
            pass_on(final, from_x, x_send, x_recv, across)
        else:
            landed(from_x, x_send, x_recv)
            out_ref[...] = (total + wide(from_x)).astype(out_ref.dtype)
    for copy in sent:
        copy.wait_send()


def collect(parts):
    dma = pltpu.SemaphoreType.DMA
    rows = parts.shape[1:]
    vmem = lambda *lead: pltpu.VMEM(lead + rows, parts.dtype)
    return pl.pallas_call(
        collect_kernel,
        out_shape=jax.ShapeDtypeStruct(rows, jnp.bfloat16),
        in_specs=[ANY],
        out_specs=IN_VMEM,
        scratch_shapes=[
            vmem(16), vmem(16), vmem(2, 2, 4), vmem(), vmem(),
            dma(()), dma(()), dma((2, 2, 4)), dma((2, 2, 4)), dma((16,)), dma((16,)), dma((16,)),
        ],
        compiler_params=params(5, vmem_limit_bytes=40 << 20),
        name="collect",
    )(parts)


def on_device(
    tokens, segment_ids, routes, attn_gain, w_query, w_key, w_value, w_out,
    moe_gain, w_router, w_gate, w_up, w_down,
):
    tp_rank = lax.axis_index("tp")
    seq_rank = lax.axis_index("seq")
    tok_dev, width = tokens.shape
    tok_seq = tok_dev * 8
    bf16, f32 = jnp.bfloat16, jnp.float32
    block_first = seq_rank * tok_seq

    seg_row = jnp.pad(segment_ids, (0, HD - tok_dev), constant_values=-1).reshape(1, HD)
    wide, segs = tp_gather(tokens, seg_row)

    block_index = block_first + jnp.arange(tok_seq, dtype=jnp.int32)
    near = segs[:, :, 0, :tok_dev].reshape(9, tok_seq)
    near_index = block_index[None, :] - tok_seq * jnp.arange(9, dtype=jnp.int32)[:, None]
    labels = jnp.arange(6, dtype=jnp.int32)
    hits = (near[None] == labels[:, None, None]) & (near_index >= 0)[None]
    firsts = jnp.min(jnp.where(hits, near_index[None], 1 << 30), axis=(1, 2))
    starts = jnp.sum(jnp.where(near[0][:, None] == labels[None, :], firsts[None, :], 0), axis=1)
    position = (block_index - starts).astype(f32)
    inverse = ROTARY ** (-(jnp.arange(HD // 2, dtype=f32) * 2.0 / HD))
    angle = position[:, None] * inverse[None, :]
    cosine, sine = jnp.cos(angle), jnp.sin(angle)

    normed = rms_rows(wide.reshape(tok_seq, width), attn_gain).astype(bf16)
    query = rotate(jnp.dot(normed, w_query, preferred_element_type=f32), cosine, sine).astype(bf16)
    keys = rotate(jnp.dot(normed, w_key, preferred_element_type=f32), cosine, sine).astype(bf16)
    values = jnp.dot(normed, w_value, preferred_element_type=f32).astype(bf16)

    def own_rows(matrix):
        mine = lax.dynamic_slice_in_dim(matrix, tp_rank * tok_dev, tok_dev, 0)
        return jnp.transpose(mine.reshape(tok_dev, KVH, HD), (1, 0, 2))

    kv_cache = jnp.stack([own_rows(keys), own_rows(values)])
    head = tp_rank // 4
    kv_own = jnp.stack(
        [
            lax.dynamic_slice_in_dim(m, head * HD, HD, 1).reshape(4, tok_seq // 4, HD)
            for m in (keys, values)
        ],
        axis=1,
    )
    resid, payload = attention_layer(
        kv_own, query, starts[:, None], tokens, w_out, moe_gain[None], w_router, routes
    )
    arrived = spread(payload).reshape(32 * tok_dev, width + HD)
    my_gates = lax.dynamic_slice_in_dim(arrived[:, width:], seq_rank, 1, 1)[:, 0]
    routed = (my_gates != 0).reshape(16, HD)
    ones = routed.astype(bf16)
    upto = jnp.arange(HD)[:, None] <= jnp.arange(HD)[None, :]
    inside = jnp.dot(ones, upto.astype(bf16), preferred_element_type=f32)
    sums = inside[:, -1]
    before = jnp.sum(jnp.where(jnp.arange(16)[None, :] < jnp.arange(16)[:, None], sums[None, :], 0.0), axis=1)
    slots = jnp.where(routed, (inside + before[:, None]).astype(jnp.int32) - 1, -1)
    total = jnp.sum(sums).astype(jnp.int32)
    info = jnp.stack([seq_rank.astype(jnp.int32), total])
    parts = run_expert(
        info, arrived, slots.reshape(1, -1), slots.reshape(-1, 1), w_gate[0], w_up[0], w_down[0]
    )
    moe = collect(parts.reshape(32, tok_dev, width))
    layer_out = (resid + moe.astype(f32)).astype(bf16)
    return (layer_out, kv_cache)


def solution(mesh):
    placed = (
        P(("seq", "tp"), None),
        P(("seq", "tp")),
        P(("seq", "tp"), None),
        P(),
        P(None, "tp"),
        P(),
        P(),
        P("tp", None),
        P(),
        P(),
        P("seq", None, None),
        P("seq", None, None),
        P("seq", None, None),
    )
    return jax.shard_map(
        on_device,
        mesh=mesh,
        in_specs=placed,
        out_specs=(P(("seq", "tp"), None), P(None, None, ("seq", "tp"), None)),
        check_vma=False,
    )
```

```python
import functools
import math

import jax
import jax.numpy as jnp
from jax import lax
from jax.experimental import pallas as pl
from jax.experimental.pallas import tpu as pltpu
from jax.sharding import PartitionSpec as P

HD = 128
QH = 8
KVH = 2
ROTARY = 1000000.0
NEGATIVE = -1e30
MESH = pl.DeviceIdType.MESH
ANY = pl.BlockSpec(memory_space=pl.ANY)
IN_VMEM = pl.BlockSpec(memory_space=pltpu.VMEM)


def rms_rows(values_in, gain):
    wide = values_in.astype(jnp.float32)
    scale = lax.rsqrt(jnp.mean(wide * wide, axis=-1, keepdims=True) + 1e-06)
    return wide * scale * gain


def rotate(matrix, cosine, sine):
    count = matrix.shape[0]
    shaped = matrix.reshape(count, -1, HD)
    half = HD // 2
    cosine, sine = cosine[:, None, :], sine[:, None, :]
    first = shaped[..., :half]
    second = shaped[..., half:]
    turned = jnp.concatenate(
        [first * cosine - second * sine, second * cosine + first * sine], axis=-1
    )
    return turned.reshape(count, -1)


def greet(peers):
    barrier = pltpu.get_barrier_semaphore()
    for peer in peers:
        pl.semaphore_signal(barrier, inc=1, device_id=peer, device_id_type=MESH)
    pl.semaphore_wait(barrier, len(peers))


def places():
    s, t = lax.axis_index("seq"), lax.axis_index("tp")
    return s, t, s // 16, (s // 2) % 8, s % 2, t // 4, t % 4


def params(number, **more):
    return pltpu.CompilerParams(collective_id=number, has_side_effects=True, **more)


class Copies:
    def __init__(self, anyone):
        self.anyone, self.sent = anyone, []

    def start(self, src, dst, send, recv, peer):
        copy = pltpu.make_async_remote_copy(
            src_ref=src, dst_ref=dst, send_sem=send, recv_sem=recv,
            device_id=peer, device_id_type=MESH,
        )
        copy.start()
        self.sent.append(copy)

    def landed(self, dst, send, recv):
        pltpu.make_async_remote_copy(
            src_ref=dst, dst_ref=dst, send_sem=send, recv_sem=recv,
            device_id=self.anyone, device_id_type=MESH,
        ).wait_recv()

    def drain(self):
        for copy in self.sent:
            copy.wait_send()


def tp_gather_kernel(
    rows_ref, seg_ref, out, segs_ref,
    send, recv, seg_send, seg_recv, far_send, far_recv, local,
):
    s, t, _, _, core, x, y = places()
    across = (1 - x) * 4
    own = x * 4
    up, down, two = (y + 1) % 4, (y + 3) % 4, (y + 2) % 4
    xp, yn, yp = (s, across + y), (s, own + up), (s, own + down)
    tp_peers = [(s, (t + k) % 8) for k in range(1, 8)]
    ahead = [((s + k) % 32, t) for k in range(1, 9)]
    behind = [((s + 32 - k) % 32, t) for k in range(1, 9)]
    greet(tp_peers + ahead + behind)
    moves = Copies(xp)

    def go(number, src, dst, peer):
        moves.start(src, dst, send.at[number], recv.at[number], peer)

    def landed(number, dst):
        moves.landed(dst, send.at[number], recv.at[number])

    seg_own = pltpu.make_async_copy(seg_ref, segs_ref.at[0, t], local.at[0])
    seg_own.start()
    for k, peer in enumerate(tp_peers):
        moves.start(seg_ref, segs_ref.at[0, t], seg_send.at[k], seg_recv.at[k], peer)
    go(0, rows_ref, out.at[t], xp)
    go(1, rows_ref, out.at[t], yn)
    go(2, rows_ref, out.at[t], yp)
    rows_own = pltpu.make_async_copy(rows_ref, out.at[t], local.at[1])
    rows_own.start()
    seg_own.wait()
    for k in range(7):
        moves.landed(segs_ref.at[0, t], seg_send.at[k], seg_recv.at[k])
    for k, peer in enumerate(ahead):
        moves.start(segs_ref.at[0], segs_ref.at[k + 1], far_send.at[k], far_recv.at[k], peer)
    low, high = pl.ds(0, 32), pl.ds(32, 32)
    landed(0, out.at[across + y])
    go(3, out.at[across + y], out.at[across + y], yn)
    go(4, out.at[across + y], out.at[across + y], yp)
    landed(1, out.at[own + down])
    go(5, out.at[own + down, low], out.at[own + down, low], yn)
    landed(2, out.at[own + up])
    go(6, out.at[own + up, high], out.at[own + up, high], yp)
    landed(3, out.at[across + down])
    go(7, out.at[across + down, low], out.at[across + down, low], yn)
    landed(4, out.at[across + up])
    go(8, out.at[across + up, high], out.at[across + up, high], yp)
    landed(5, out.at[own + two, low])
    landed(6, out.at[own + two, high])
    landed(7, out.at[across + two, low])
    landed(8, out.at[across + two, high])
    rows_own.wait()
    for k in range(8):
        moves.landed(segs_ref.at[k + 1], far_send.at[k], far_recv.at[k])
    moves.drain()


def tp_gather(rows, seg):
    count, width = rows.shape
    dma = pltpu.SemaphoreType.DMA
    return pl.pallas_call(
        tp_gather_kernel,
        out_shape=(
            jax.ShapeDtypeStruct((8, count, width), rows.dtype),
            jax.ShapeDtypeStruct((9, 8, 1, 128), jnp.int32),
        ),
        in_specs=[IN_VMEM] * 2,
        out_specs=(IN_VMEM,) * 2,
        scratch_shapes=[dma((9,)), dma((9,)), dma((7,)), dma((7,)), dma((8,)), dma((8,)), dma((2,))],
        compiler_params=params(1, vmem_limit_bytes=16 << 20),
        name="tp_gather",
    )(rows, seg)


TILE = 128


def attention_kernel(
    kv_ref, q_ref, start_ref, tokens_ref, w_out_ref, gain_ref, router_ref, routes_ref,
    resid_ref, payload_ref,
    slots, w_full, peak, total, mixed, heads_out, heads_in,
    z_send, z_recv, y_send, y_recv, c_send, c_recv,
    w_send, w_recv, t_send, t_recv, h_send, h_recv, local,
):
    s, t, _, _, core, x, y = places()
    across, own = (1 - x) * 4, x * 4
    up, down, two = (y + 1) % 4, (y + 3) % 4, (y + 2) % 4
    far = ((s + 4) % 32, t)
    near = ((s + 2) % 32, t)
    xp, yn, yp = (s, across + y), (s, own + up), (s, own + down)
    twin = (s + 1 - 2 * core, t)
    tp_peers = [(s, (t + k) % 8) for k in range(1, 8)]
    greet(tp_peers + [twin, near, far, ((s + 30) % 32, t), ((s + 28) % 32, t)])
    moves = Copies(twin)
    count = q_ref.shape[0]

    def w_piece(rank, half, first=0, rows=64):
        return w_full.at[rank, pl.ds(pl.multiple_of(half * 64 + first, 32), rows)]

    def w_go(number, rank, peer, first=0, rows=64):
        piece = w_piece(rank, core, first, rows)
        moves.start(piece, piece, w_send.at[number], w_recv.at[number], peer)

    def w_landed(number, rank, first=0, rows=64):
        moves.landed(w_piece(rank, core, first, rows), w_send.at[number], w_recv.at[number])

    def w_twin(number, rank):
        piece = w_piece(rank, core)
        moves.start(piece, piece, t_send.at[number], t_recv.at[number], twin)

    kv_own = pltpu.make_async_copy(kv_ref, slots.at[0], local.at[0])
    kv_own.start()
    w_own = pltpu.make_async_copy(w_out_ref, w_full.at[t], local.at[1])
    w_own.start()
    moves.start(kv_ref.at[y], slots.at[2, y], z_send.at[0], z_recv.at[0], near)
    moves.start(kv_ref.at[y], slots.at[4, y], z_send.at[1], z_recv.at[1], far)
    w_own.wait()
    w_go(0, t, xp)
    w_go(1, t, yn)
    w_go(2, t, yp)

    peak[...] = jnp.full_like(peak, NEGATIVE)
    total[...] = jnp.zeros_like(total)
    mixed[...] = jnp.zeros_like(mixed)
    base = s * count
    unit = math.log2(math.e) / math.sqrt(HD)

    def attend(j):
        def tile(number, _):
            rows = pl.ds(pl.multiple_of(number * TILE, TILE), TILE)
            keys = slots[j, :, 0].reshape(count, HD)
            values = slots[j, :, 1].reshape(count, HD)
            scores = lax.dot_general(
                q_ref[rows, :], keys, (((1,), (1,)), ((), ())), preferred_element_type=jnp.float32
            ) * unit
            key_index = base - j * count + lax.broadcasted_iota(jnp.int32, (1, count), 1)
            allowed = key_index >= start_ref[rows, :]
            if j == 0:
                query_index = base + number * TILE + lax.broadcasted_iota(jnp.int32, (TILE, 1), 0)
                allowed = allowed & (key_index <= query_index)
            masked = jnp.where(allowed, scores, NEGATIVE)
            old = peak[rows, :]
            newest = jnp.maximum(old, jnp.max(masked, axis=-1, keepdims=True))
            factor = jnp.exp2(old - newest)
            weights = jnp.exp2(masked - newest)
            total[rows, :] = total[rows, :] * factor + jnp.sum(weights, axis=-1, keepdims=True)
            mixed[rows, :] = mixed[rows, :] * factor + jnp.dot(
                weights.astype(jnp.bfloat16), values, preferred_element_type=jnp.float32
            )
            peak[rows, :] = newest
            return 0

        lax.fori_loop(0, count // TILE, tile, 0)

    def z_step(k, onward):
        piece = slots.at[2 * k, y]
        moves.landed(piece, z_send.at[k - 1], z_recv.at[k - 1])
        if onward:
            moves.start(piece, slots.at[2 * k + 4, y], z_send.at[k + 1], z_recv.at[k + 1], far)
        moves.start(piece, piece, y_send.at[k - 1, 0], y_recv.at[k - 1, 0], yn)
        moves.start(piece, piece, y_send.at[k - 1, 1], y_recv.at[k - 1, 1], yp)

    def y_step(k):
        moves.landed(slots.at[2 * k, down], y_send.at[k - 1, 0], y_recv.at[k - 1, 0])
        piece = slots.at[2 * k, down, 0]
        moves.start(piece, piece, y_send.at[k - 1, 2], y_recv.at[k - 1, 2], yn)
        moves.landed(slots.at[2 * k, up], y_send.at[k - 1, 1], y_recv.at[k - 1, 1])
        piece = slots.at[2 * k, up, 1]
        moves.start(piece, piece, y_send.at[k - 1, 3], y_recv.at[k - 1, 3], yp)

    def block_step(k):
        moves.landed(slots.at[2 * k, two, 0], y_send.at[k - 1, 2], y_recv.at[k - 1, 2])
        moves.landed(slots.at[2 * k, two, 1], y_send.at[k - 1, 3], y_recv.at[k - 1, 3])
        moves.start(
            slots.at[2 * k - 2 + 2 * core], slots.at[2 * k - 1], c_send.at[k - 1], c_recv.at[k - 1], twin
        )

    def twin_step(k):
        moves.landed(slots.at[2 * k - 1], c_send.at[k - 1], c_recv.at[k - 1])
        attend(2 * k - 1)

    kv_own.wait()
    attend(0)
    z_step(1, True)
    z_step(2, True)
    w_landed(0, across + y)
    w_go(3, across + y, yn)
    w_go(4, across + y, yp)
    w_twin(0, across + y)
    y_step(1)
    y_step(2)
    w_landed(1, own + down)
    w_go(5, own + down, yn, 0, 32)
    w_twin(1, own + down)
    w_landed(2, own + up)
    w_go(6, own + up, yp, 32, 32)
    w_twin(2, own + up)
    block_step(1)
    attend(2)
    z_step(3, False)
    z_step(4, False)
    block_step(2)
    twin_step(1)
    y_step(3)
    y_step(4)
    attend(4)
    w_landed(3, across + down)
    w_go(7, across + down, yn, 0, 32)
    w_twin(3, across + down)
    w_landed(4, across + up)
    w_go(8, across + up, yp, 32, 32)
    w_twin(4, across + up)
    block_step(3)
    twin_step(2)
    block_step(4)
    attend(6)
    twin_step(3)
    w_landed(5, own + two, 0, 32)
    w_landed(6, own + two, 32, 32)
    w_twin(5, own + two)
    attend(8)
    w_landed(7, across + two, 0, 32)
    w_landed(8, across + two, 32, 32)
    w_twin(6, across + two)
    twin_step(4)

    for rank in range(8):
        rows = pl.ds(rank * 64, 64)
        heads_out[rank] = (mixed[rows, :] / total[rows, :]).astype(heads_out.dtype)
    heads_own = pltpu.make_async_copy(heads_out.at[t], heads_in.at[t], local.at[0])
    heads_own.start()
    for k, peer in enumerate(tp_peers):
        moves.start(heads_out.at[peer[1]], heads_in.at[t], h_send.at[k], h_recv.at[k], peer)
    ranks = [across + y, own + down, own + up, across + down, across + up, own + two, across + two]
    for number, rank in enumerate(ranks):
        moves.landed(w_piece(rank, 1 - core), t_send.at[number], t_recv.at[number])
    heads_own.wait()
    for k in range(7):
        moves.landed(heads_in.at[t], h_send.at[k], h_recv.at[k])
    attention = jnp.concatenate([heads_in[rank] for rank in range(8)], axis=1)
    width = tokens_ref.shape[1]
    resid = tokens_ref[...].astype(jnp.float32) + jnp.dot(
        attention, w_full[...].reshape(8 * HD, width), preferred_element_type=jnp.float32
    )
    resid_ref[...] = resid
    moe_rows = rms_rows(resid, gain_ref[...]).astype(jnp.bfloat16)
    payload_ref[:, :width] = moe_rows
    logits = jnp.dot(moe_rows, router_ref[...], preferred_element_type=jnp.float32)
    experts = logits.shape[1]
    expert_ids = lax.broadcasted_iota(jnp.int32, logits.shape, 1)
    routes = routes_ref[...]
    picked = [routes[:, k : k + 1] == expert_ids for k in range(routes.shape[1])]
    chosen = [jnp.sum(jnp.where(one, logits, 0.0), axis=1, keepdims=True) for one in picked]
    highest = functools.reduce(jnp.maximum, chosen)
    powers = [jnp.exp(one - highest) for one in chosen]
    whole = functools.reduce(jnp.add, powers)
    table = jnp.zeros_like(logits)
    for one, power in zip(picked, powers):
        table = jnp.where(one, power / whole, table)
    payload_ref[:, width:] = jnp.zeros((logits.shape[0], HD), jnp.bfloat16)
    payload_ref[:, width : width + experts] = table.astype(jnp.bfloat16)
    moves.drain()


def attention_layer(kv, query, starts, tokens, w_out, gain, router, routes):
    dma = pltpu.SemaphoreType.DMA
    bf16, f32 = jnp.bfloat16, jnp.float32
    rows, width = tokens.shape
    count = query.shape[0]
    return pl.pallas_call(
        attention_kernel,
        out_shape=(
            jax.ShapeDtypeStruct((rows, width), f32),
            jax.ShapeDtypeStruct((rows, width + HD), bf16),
        ),
        in_specs=[IN_VMEM] * 8,
        out_specs=(IN_VMEM,) * 2,
        scratch_shapes=[
            pltpu.VMEM((9,) + kv.shape, bf16),
            pltpu.VMEM((8, HD, width), bf16),
            pltpu.VMEM((count, 1), f32),
            pltpu.VMEM((count, 1), f32),
            pltpu.VMEM((count, HD), f32),
            pltpu.VMEM((8, rows, HD), bf16),
            pltpu.VMEM((8, rows, HD), bf16),
            dma((4,)), dma((4,)), dma((4, 4)), dma((4, 4)), dma((4,)), dma((4,)),
            dma((9,)), dma((9,)), dma((7,)), dma((7,)), dma((7,)), dma((7,)), dma((2,)),
        ],
        compiler_params=params(2, vmem_limit_bytes=32 << 20),
        name="attention_layer",
    )(kv, query, starts, tokens, w_out, gain, router, routes)


HALF = 32


def ring_places():
    s, t, plane, z, core, x, y = places()
    across = ((1 - plane) * 16 + z * 2 + core, (1 - x) * 4 + y)
    twin = (s + 1 - 2 * core, t)
    ring = [(plane * 16 + ((z + d) % 8) * 2 + core, t) for d in (1, 7)]
    return s, z, core, [plane, 1 - plane], across, twin, ring


def spread_kernel(
    rows_ref, out_ref, ax_send, ax_recv, az_send, az_recv,
    bx_send, bx_recv, bz_send, bz_recv, c_send, c_recv, local,
):
    s, z, core, planes, across, twin, ring = ring_places()
    greet([across, twin] + ring)
    moves = Copies(twin)
    part_a, part_b = pl.ds(0, HALF), pl.ds(HALF, HALF)
    quarters = [pl.ds(HALF, HALF // 2), pl.ds(HALF + HALF // 2, HALF // 2)]

    def slot(p, way, distance):
        back = (z + 8 - distance) % 8 if way == 0 else (z + distance) % 8
        return planes[p] * 16 + back * 2 + core

    twins = []

    def to_twin(src, block, part):
        k = len(twins)
        twins.append(part)
        moves.start(src, out_ref.at[block, part], c_send.at[k], c_recv.at[k], twin)

    crossed = []

    def cross(src, block):
        k = len(crossed)
        crossed.append(k)
        moves.start(src, out_ref.at[block, part_b], bx_send.at[k], bx_recv.at[k], across)

    def a_travels(p, way, distance):
        return distance <= 3 or (distance == 4 and p == way)

    def a_arrives(p, way, distance):
        if not a_travels(p, way, distance):
            return
        block, k = slot(p, way, distance), distance - 1
        piece = out_ref.at[block, part_a]
        moves.landed(piece, az_send.at[p, way, k], az_recv.at[p, way, k])
        if a_travels(p, way, distance + 1):
            moves.start(piece, piece, az_send.at[p, way, k + 1], az_recv.at[p, way, k + 1], ring[way])
        to_twin(piece, block, part_a)

    def b_arrives(way, distance):
        block, k = slot(0, way, distance), distance - 1
        if distance == 4:
            piece = out_ref.at[block, quarters[way]]
            moves.landed(piece, bz_send.at[way, k], bz_recv.at[way, k])
            if way == 0:
                return
        piece = out_ref.at[block, part_b]
        if distance < 4:
            moves.landed(piece, bz_send.at[way, k], bz_recv.at[way, k])
            onward = out_ref.at[block, quarters[way]] if distance == 3 else piece
            moves.start(onward, onward, bz_send.at[way, k + 1], bz_recv.at[way, k + 1], ring[way])
        cross(piece, block)
        to_twin(piece, block, part_b)

    def b_crossed(k, way, distance):
        block = slot(1, way, distance)
        piece = out_ref.at[block, part_b]
        moves.landed(piece, bx_send.at[k], bx_recv.at[k])
        to_twin(piece, block, part_b)

    own = pltpu.make_async_copy(rows_ref, out_ref.at[s], local)
    own.start()
    own_a, own_b = rows_ref.at[part_a], rows_ref.at[part_b]
    moves.start(own_a, out_ref.at[s, part_a], ax_send, ax_recv, across)
    for way in range(2):
        moves.start(own_b, out_ref.at[s, part_b], bz_send.at[way, 0], bz_recv.at[way, 0], ring[way])
    for way in range(2):
        moves.start(own_a, out_ref.at[s, part_a], az_send.at[0, way, 0], az_recv.at[0, way, 0], ring[way])
    cross(own_b, s)
    to_twin(own_a, s, part_a)
    to_twin(own_b, s, part_b)
    block = across[0]
    piece = out_ref.at[block, part_a]
    moves.landed(piece, ax_send, ax_recv)
    for way in range(2):
        moves.start(piece, piece, az_send.at[1, way, 0], az_recv.at[1, way, 0], ring[way])
    to_twin(piece, block, part_a)
    for distance in range(1, 5):
        for way in range(2):
            b_arrives(way, distance)
        for p in range(2):
            for way in range(2):
                a_arrives(p, way, distance)
        if distance == 1:
            b_crossed(0, 0, 0)
        else:
            b_crossed(2 * distance - 3, 0, distance - 1)
            b_crossed(2 * distance - 2, 1, distance - 1)
    b_crossed(7, 0, 4)
    own.wait()
    for k, part in enumerate(twins):
        moves.landed(out_ref.at[twin[0], part], c_send.at[k], c_recv.at[k])
    moves.drain()


def spread(rows):
    dma = pltpu.SemaphoreType.DMA
    return pl.pallas_call(
        spread_kernel,
        out_shape=jax.ShapeDtypeStruct((32,) + rows.shape, rows.dtype),
        in_specs=[IN_VMEM],
        out_specs=IN_VMEM,
        scratch_shapes=[
            dma(()), dma(()), dma((2, 2, 4)), dma((2, 2, 4)), dma((8,)), dma((8,)),
            dma((2, 4)), dma((2, 4)), dma((32,)), dma((32,)), dma(()),
        ],
        compiler_params=params(4, vmem_limit_bytes=12 << 20),
        name="spread",
    )(rows)


CHUNK = 256


def expert_kernel(rows_ref, gate_ref, up_ref, down_ref, out_ref, column, lane, gathered, contribution, starts):
    width = gate_ref.shape[0]
    blocks = rows_ref.shape[0] // CHUNK
    expert = lax.axis_index("seq")
    bf16, f32 = jnp.bfloat16, jnp.float32
    down_index = lax.broadcasted_iota(jnp.int32, (CHUNK, CHUNK), 0)
    along_index = lax.broadcasted_iota(jnp.int32, (CHUNK, CHUNK), 1)
    zero_first = (((0,), (0,)), ((), ()))

    def span(block):
        return pl.ds(pl.multiple_of(block * CHUNK, CHUNK), CHUNK)

    def number_rows(block, before):
        routed = (rows_ref[span(block), width:].astype(f32) != 0.0).astype(f32)
        here = lax.broadcasted_iota(jnp.int32, routed.shape, 1) == expert
        routed = jnp.where(here, routed, 0.0)
        ones = routed.astype(bf16)
        upto = jnp.dot((along_index <= down_index).astype(f32).astype(bf16), ones, preferred_element_type=f32)
        hit = jnp.sum(routed, axis=1, keepdims=True)
        rank = jnp.sum(jnp.where(here, upto, 0.0), axis=1, keepdims=True)
        column[span(block), :] = jnp.where(hit > 0.0, rank + (before - 1.0), -1.0)
        upto = lax.dot_general(
            ones, (down_index <= along_index).astype(f32).astype(bf16), zero_first, preferred_element_type=f32
        )
        same = lax.dot_general(
            ones, (down_index == along_index).astype(f32).astype(bf16), zero_first, preferred_element_type=f32
        )
        hit = jnp.sum(same, axis=0, keepdims=True)
        mine = lax.broadcasted_iota(jnp.int32, upto.shape, 0) == expert
        rank = jnp.sum(jnp.where(mine, upto, 0.0), axis=0, keepdims=True)
        lane[block] = jnp.where(hit > 0.0, rank + (before - 1.0), -1.0)
        starts[block] = before.astype(jnp.int32)
        return before + jnp.sum(routed)

    routed = lax.fori_loop(0, blocks, number_rows, jnp.float32(0.0)).astype(jnp.int32)
    starts[blocks] = routed

    def one_chunk(number, _):
        base = number * CHUNK
        gathered[...] = jnp.zeros_like(gathered)

        def touches(block):
            first, end = starts[block], starts[block + 1]
            return (first < base + CHUNK) & ((end > base) | (first >= base))

        def gather(block, _):
            @pl.when(touches(block))
            def _():
                slots = base + lax.broadcasted_iota(jnp.int32, (CHUNK, 1), 0)
                picks = (lane[block] == slots.astype(f32)).astype(f32).astype(bf16)
                gathered[...] += jnp.dot(picks, rows_ref[span(block), :], preferred_element_type=f32)

            return 0

        lax.fori_loop(0, blocks, gather, 0)
        all_gates = gathered[:, width:]
        here = lax.broadcasted_iota(jnp.int32, all_gates.shape, 1) == expert
        gates = jnp.sum(jnp.where(here, all_gates, 0.0), axis=1, keepdims=True)
        rows = gathered[:, :width].astype(bf16)
        gate_out = jnp.dot(rows, gate_ref[...], preferred_element_type=f32)
        up_out = jnp.dot(rows, up_ref[...], preferred_element_type=f32)
        active = (jnp.maximum(gate_out, 0.0) * up_out).astype(bf16)
        down_out = jnp.dot(active, down_ref[...], preferred_element_type=f32) * gates
        contribution[...] = down_out.astype(bf16)

        def place(block, _):
            @pl.when(touches(block))
            def _():
                slots = base + lax.broadcasted_iota(jnp.int32, (1, CHUNK), 1)
                back = (column[span(block), :] == slots.astype(f32)).astype(f32).astype(bf16)
                placed = jnp.dot(back, contribution[...], preferred_element_type=f32)

                @pl.when(starts[block] >= base)
                def _():
                    out_ref[span(block), :] = placed.astype(bf16)

                @pl.when(starts[block] < base)
                def _():
                    out_ref[span(block), :] = (out_ref[span(block), :].astype(f32) + placed).astype(bf16)

            return 0

        lax.fori_loop(0, blocks, place, 0)
        return 0

    lax.fori_loop(0, routed // CHUNK + 1, one_chunk, 0)


def run_expert(rows, w_gate, w_up, w_down):
    tokens, columns = rows.shape
    width = w_gate.shape[0]
    return pl.pallas_call(
        expert_kernel,
        out_shape=jax.ShapeDtypeStruct((tokens, width), jnp.bfloat16),
        in_specs=[IN_VMEM] * 4,
        out_specs=IN_VMEM,
        scratch_shapes=[
            pltpu.VMEM((tokens, 1), jnp.float32),
            pltpu.VMEM((tokens // CHUNK, 1, CHUNK), jnp.float32),
            pltpu.VMEM((CHUNK, columns), jnp.float32),
            pltpu.VMEM((CHUNK, width), jnp.bfloat16),
            pltpu.SMEM((tokens // CHUNK + 1,), jnp.int32),
        ],
        compiler_params=pltpu.CompilerParams(vmem_limit_bytes=28 << 20),
        name="run_expert",
    )(rows, w_gate, w_up, w_down)


def collect_kernel(
    in_ref, out_ref, other, total_a, total_b, a_in, b_in, bx_in, from_x,
    ax_send, ax_recv, az_send, az_recv, bx_send, bx_recv, bz_send, bz_recv, c_send, c_recv,
):
    s, z, core, planes, across, twin, ring = ring_places()
    greet([across, twin] + ring)
    moves = Copies(twin)
    part_a, part_b = pl.ds(0, HALF), pl.ds(HALF, HALF)
    quarters = [pl.ds(0, HALF // 2), pl.ds(HALF // 2, HALF // 2)]
    wide = lambda values: values.astype(jnp.float32)

    def place(p, way, distance):
        ahead = (z + distance) % 8 if way == 0 else (z + 8 - distance) % 8
        return ahead, planes[p] * 8 + ahead

    order = [(1, 0, 4), (0, 0, 4)]
    for distance in (3, 2, 1):
        order += [(p, way, distance) for p in (1, 0) for way in range(2)]
    order += [(1, 0, 0), (0, 0, 0)]
    for k, key in enumerate(order):
        _, i = place(*key)
        moves.start(in_ref.at[2 * i + 1 - core], other.at[i], c_send.at[k], c_recv.at[k], twin)

    crossed = {}
    for k, (p, way, distance) in enumerate(order):
        ahead, i = place(p, way, distance)
        moves.landed(other.at[i], c_send.at[k], c_recv.at[k])

        mine = wide(in_ref[2 * i + core, part_b]) + wide(other[i, part_b])
        if p == 1:
            total_b[i] = mine.astype(jnp.bfloat16)
            j = len(crossed)
            crossed[way, distance] = j
            moves.start(total_b.at[i], bx_in.at[ahead], bx_send.at[j], bx_recv.at[j], across)

        ours = wide(in_ref[2 * i + core, part_a]) + wide(other[i, part_a])
        if distance > 0:
            ways = [p] if distance == 4 else [way]
            for w in ways:
                if distance < (4 if p == w else 3):
                    piece = a_in.at[p, w, distance]
                    moves.landed(piece, az_send.at[p, w, distance], az_recv.at[p, w, distance])
                    ours = ours + wide(piece[...])
                total_a[i] = ours.astype(jnp.bfloat16)
                moves.start(
                    total_a.at[i], a_in.at[p, w, distance - 1],
                    az_send.at[p, w, distance - 1], az_recv.at[p, w, distance - 1], ring[w],
                )
        else:
            for w in range(2):
                piece = a_in.at[p, w, 0]
                moves.landed(piece, az_send.at[p, w, 0], az_recv.at[p, w, 0])
                ours = ours + wide(piece[...])
            if p == 1:
                total_a[i] = ours.astype(jnp.bfloat16)
                moves.start(total_a.at[i], from_x, ax_send, ax_recv, across)

        if p == 0:
            j = crossed[way, distance]
            moves.landed(bx_in.at[ahead], bx_send.at[j], bx_recv.at[j])
            mine = mine + wide(bx_in[ahead])
            if distance == 4:
                total_b[i] = mine.astype(jnp.bfloat16)
                for w in range(2):
                    moves.start(
                        total_b.at[i, quarters[w]], b_in.at[w, 3, quarters[w]],
                        bz_send.at[w, 3], bz_recv.at[w, 3], ring[w],
                    )
            elif distance == 3:
                piece = b_in.at[way, 3, quarters[way]]
                moves.landed(piece, bz_send.at[way, 3], bz_recv.at[way, 3])
                split = HALF // 2
                first, second = mine[:split], mine[split:]
                if way == 0:
                    first = first + wide(piece[...])
                else:
                    second = second + wide(piece[...])
                total_b[i, quarters[0]] = first.astype(jnp.bfloat16)
                total_b[i, quarters[1]] = second.astype(jnp.bfloat16)
            elif distance > 0:
                piece = b_in.at[way, distance]
                moves.landed(piece, bz_send.at[way, distance], bz_recv.at[way, distance])
                total_b[i] = (mine + wide(piece[...])).astype(jnp.bfloat16)
            if 0 < distance < 4:
                moves.start(
                    total_b.at[i], b_in.at[way, distance - 1],
                    bz_send.at[way, distance - 1], bz_recv.at[way, distance - 1], ring[way],
                )
            if distance == 0:
                for w in range(2):
                    piece = b_in.at[w, 0]
                    moves.landed(piece, bz_send.at[w, 0], bz_recv.at[w, 0])
                    mine = mine + wide(piece[...])
                out_ref[part_b, :] = mine.astype(out_ref.dtype)
                moves.landed(from_x, ax_send, ax_recv)
                out_ref[part_a, :] = (ours + wide(from_x[...])).astype(out_ref.dtype)
    moves.drain()


def collect(parts):
    dma = pltpu.SemaphoreType.DMA
    _, rows, width = parts.shape
    vmem = lambda *lead: pltpu.VMEM(lead + (width,), parts.dtype)
    return pl.pallas_call(
        collect_kernel,
        out_shape=jax.ShapeDtypeStruct((rows, width), jnp.bfloat16),
        in_specs=[IN_VMEM],
        out_specs=IN_VMEM,
        scratch_shapes=[
            vmem(16, rows), vmem(16, HALF), vmem(16, HALF), vmem(2, 2, 4, HALF), vmem(2, 4, HALF),
            vmem(8, HALF), vmem(HALF),
            dma(()), dma(()), dma((2, 2, 4)), dma((2, 2, 4)), dma((8,)), dma((8,)),
            dma((2, 4)), dma((2, 4)), dma((16,)), dma((16,)),
        ],
        compiler_params=params(5, vmem_limit_bytes=28 << 20),
        name="collect",
    )(parts)


def on_device(
    tokens, segment_ids, routes, attn_gain, w_query, w_key, w_value, w_out,
    moe_gain, w_router, w_gate, w_up, w_down,
):
    tp_rank = lax.axis_index("tp")
    seq_rank = lax.axis_index("seq")
    tok_dev, width = tokens.shape
    tok_seq = tok_dev * 8
    bf16, f32 = jnp.bfloat16, jnp.float32
    block_first = seq_rank * tok_seq

    seg_row = jnp.pad(segment_ids, (0, HD - tok_dev), constant_values=-1).reshape(1, HD)
    wide, segs = tp_gather(tokens, seg_row)

    block_index = block_first + jnp.arange(tok_seq, dtype=jnp.int32)
    near = segs[:, :, 0, :tok_dev].reshape(9, tok_seq)
    near_index = block_index[None, :] - tok_seq * jnp.arange(9, dtype=jnp.int32)[:, None]
    labels = jnp.arange(6, dtype=jnp.int32)
    hits = (near[None] == labels[:, None, None]) & (near_index >= 0)[None]
    firsts = jnp.min(jnp.where(hits, near_index[None], 1 << 30), axis=(1, 2))
    starts = jnp.sum(jnp.where(near[0][:, None] == labels[None, :], firsts[None, :], 0), axis=1)
    position = (block_index - starts).astype(f32)
    inverse = ROTARY ** (-(jnp.arange(HD // 2, dtype=f32) * 2.0 / HD))
    angle = position[:, None] * inverse[None, :]
    cosine, sine = jnp.cos(angle), jnp.sin(angle)

    normed = rms_rows(wide.reshape(tok_seq, width), attn_gain).astype(bf16)
    query = rotate(jnp.dot(normed, w_query, preferred_element_type=f32), cosine, sine).astype(bf16)
    keys = rotate(jnp.dot(normed, w_key, preferred_element_type=f32), cosine, sine).astype(bf16)
    values = jnp.dot(normed, w_value, preferred_element_type=f32).astype(bf16)

    def own_rows(matrix):
        mine = lax.dynamic_slice_in_dim(matrix, tp_rank * tok_dev, tok_dev, 0)
        return jnp.transpose(mine.reshape(tok_dev, KVH, HD), (1, 0, 2))

    kv_cache = jnp.stack([own_rows(keys), own_rows(values)])
    head = tp_rank // 4
    kv_own = jnp.stack(
        [
            lax.dynamic_slice_in_dim(m, head * HD, HD, 1).reshape(4, tok_seq // 4, HD)
            for m in (keys, values)
        ],
        axis=1,
    )
    resid, payload = attention_layer(
        kv_own, query, starts[:, None], tokens, w_out, moe_gain[None], w_router, routes
    )
    arrived = spread(payload).reshape(32 * tok_dev, width + HD)
    parts = run_expert(arrived, w_gate[0], w_up[0], w_down[0])
    moe = collect(parts.reshape(32, tok_dev, width))
    layer_out = (resid + moe.astype(f32)).astype(bf16)
    return (layer_out, kv_cache)


def solution(mesh):
    placed = (
        P(("seq", "tp"), None),
        P(("seq", "tp")),
        P(("seq", "tp"), None),
        P(),
        P(None, "tp"),
        P(),
        P(),
        P("tp", None),
        P(),
        P(),
        P("seq", None, None),
        P("seq", None, None),
        P("seq", None, None),
    )
    return jax.shard_map(
        on_device,
        mesh=mesh,
        in_specs=placed,
        out_specs=(P(("seq", "tp"), None), P(None, None, ("seq", "tp"), None)),
        check_vma=False,
    )
```

```python
import functools
import math

import jax
import jax.numpy as jnp
from jax import lax
from jax.experimental import pallas as pl
from jax.experimental.pallas import tpu as pltpu
from jax.sharding import PartitionSpec as P

HD = 128
QH = 8
KVH = 2
ROTARY = 1000000.0
NEGATIVE = -1e30
MESH = pl.DeviceIdType.MESH
ANY = pl.BlockSpec(memory_space=pl.ANY)
IN_VMEM = pl.BlockSpec(memory_space=pltpu.VMEM)


def rms_rows(values_in, gain):
    wide = values_in.astype(jnp.float32)
    scale = lax.rsqrt(jnp.mean(wide * wide, axis=-1, keepdims=True) + 1e-06)
    return wide * scale * gain


def rotate(matrix, cosine, sine):
    count = matrix.shape[0]
    shaped = matrix.reshape(count, -1, HD)
    half = HD // 2
    cosine, sine = cosine[:, None, :], sine[:, None, :]
    first = shaped[..., :half]
    second = shaped[..., half:]
    turned = jnp.concatenate(
        [first * cosine - second * sine, second * cosine + first * sine], axis=-1
    )
    return turned.reshape(count, -1)


def greet(peers):
    barrier = pltpu.get_barrier_semaphore()
    for peer in peers:
        pl.semaphore_signal(barrier, inc=1, device_id=peer, device_id_type=MESH)
    pl.semaphore_wait(barrier, len(peers))


def places():
    s, t = lax.axis_index("seq"), lax.axis_index("tp")
    return s, t, s // 16, (s // 2) % 8, s % 2, t // 4, t % 4


def params(number, **more):
    return pltpu.CompilerParams(collective_id=number, has_side_effects=True, **more)


class Copies:
    def __init__(self, anyone):
        self.anyone, self.sent = anyone, []

    def start(self, src, dst, send, recv, peer):
        copy = pltpu.make_async_remote_copy(
            src_ref=src, dst_ref=dst, send_sem=send, recv_sem=recv,
            device_id=peer, device_id_type=MESH,
        )
        copy.start()
        self.sent.append(copy)

    def landed(self, dst, send, recv):
        pltpu.make_async_remote_copy(
            src_ref=dst, dst_ref=dst, send_sem=send, recv_sem=recv,
            device_id=self.anyone, device_id_type=MESH,
        ).wait_recv()

    def drain(self):
        for copy in self.sent:
            copy.wait_send()


def tp_gather_kernel(
    rows_ref, seg_ref, w_ref, out, segs_ref, w_full,
    send, recv, seg_send, seg_recv, far_send, far_recv,
    wp_send, wp_recv, wz_send, wz_recv, wt_send, wt_recv, local,
):
    s, t, plane, z, core, x, y = places()
    across = (1 - x) * 4
    own = x * 4
    up, down, two = (y + 1) % 4, (y + 3) % 4, (y + 2) % 4
    xp, yn, yp = (s, across + y), (s, own + up), (s, own + down)
    tp_peers = [(s, (t + k) % 8) for k in range(1, 8)]
    ahead = [((s + k) % 32, t) for k in range(1, 9)]
    behind = [((s + 32 - k) % 32, t) for k in range(1, 9)]
    twin = (s + 1 - 2 * core, t)
    ring = [(plane * 16 + ((z + d) % 8) * 2 + core, t) for d in (1, 7)]
    greet(tp_peers + ahead + behind + ring + [twin])
    moves = Copies(xp)
    sub = 2 * z + core
    lanes = [pl.ds(0, 4), pl.ds(4, 4)]
    twins = []

    def w_twin(back):
        k = len(twins)
        twins.append(k)
        piece = w_full.at[:, 2 * back + core]
        moves.start(piece, piece, wt_send.at[k], wt_recv.at[k], twin)

    def w_step(distance):
        for way in range(2):
            back = (z + 8 - distance) % 8 if way == 0 else (z + distance) % 8
            k = distance - 1
            span = lanes[way] if distance == 4 else slice(None)
            piece = w_full.at[span, 2 * back + core]
            moves.landed(piece, wz_send.at[way, k], wz_recv.at[way, k])
            if distance < 4:
                span = lanes[way] if distance == 3 else slice(None)
                piece = w_full.at[span, 2 * back + core]
                moves.start(piece, piece, wz_send.at[way, k + 1], wz_recv.at[way, k + 1], ring[way])
                w_twin(back)
        if distance == 4:
            w_twin((z + 4) % 8)

    def go(number, src, dst, peer):
        moves.start(src, dst, send.at[number], recv.at[number], peer)

    def landed(number, dst):
        moves.landed(dst, send.at[number], recv.at[number])

    seg_own = pltpu.make_async_copy(seg_ref, segs_ref.at[0, t], local.at[0])
    seg_own.start()
    for k, peer in enumerate(tp_peers):
        moves.start(seg_ref, segs_ref.at[0, t], seg_send.at[k], seg_recv.at[k], peer)
    go(0, rows_ref, out.at[t], xp)
    go(1, rows_ref, out.at[t], yn)
    go(2, rows_ref, out.at[t], yp)
    rows_own = pltpu.make_async_copy(rows_ref, out.at[t], local.at[1])
    rows_own.start()
    w_own = pltpu.make_async_copy(w_ref.at[sub], w_full.at[t, sub], local.at[2])
    w_own.start()
    for k, peer in enumerate(tp_peers):
        moves.start(w_ref.at[sub], w_full.at[t, sub], wp_send.at[k], wp_recv.at[k], peer)
    seg_own.wait()
    for k in range(7):
        moves.landed(segs_ref.at[0, t], seg_send.at[k], seg_recv.at[k])
    for k, peer in enumerate(ahead):
        moves.start(segs_ref.at[0], segs_ref.at[k + 1], far_send.at[k], far_recv.at[k], peer)
    low, high = pl.ds(0, 32), pl.ds(32, 32)
    landed(0, out.at[across + y])
    go(3, out.at[across + y], out.at[across + y], yn)
    go(4, out.at[across + y], out.at[across + y], yp)
    w_own.wait()
    for k in range(7):
        moves.landed(w_full.at[t, sub], wp_send.at[k], wp_recv.at[k])
    for way in range(2):
        piece = w_full.at[:, sub]
        moves.start(piece, piece, wz_send.at[way, 0], wz_recv.at[way, 0], ring[way])
    w_twin(z)
    landed(1, out.at[own + down])
    go(5, out.at[own + down, low], out.at[own + down, low], yn)
    landed(2, out.at[own + up])
    go(6, out.at[own + up, high], out.at[own + up, high], yp)
    w_step(1)
    landed(3, out.at[across + down])
    go(7, out.at[across + down, low], out.at[across + down, low], yn)
    landed(4, out.at[across + up])
    go(8, out.at[across + up, high], out.at[across + up, high], yp)
    w_step(2)
    landed(5, out.at[own + two, low])
    landed(6, out.at[own + two, high])
    landed(7, out.at[across + two, low])
    landed(8, out.at[across + two, high])
    rows_own.wait()
    w_step(3)
    w_step(4)
    for k in twins:
        moves.landed(w_full.at[:, sub], wt_send.at[k], wt_recv.at[k])
    for k in range(8):
        moves.landed(segs_ref.at[k + 1], far_send.at[k], far_recv.at[k])
    moves.drain()


def tp_gather(rows, seg, weight):
    count, width = rows.shape
    dma = pltpu.SemaphoreType.DMA
    return pl.pallas_call(
        tp_gather_kernel,
        out_shape=(
            jax.ShapeDtypeStruct((8, count, width), rows.dtype),
            jax.ShapeDtypeStruct((9, 8, 1, 128), jnp.int32),
            jax.ShapeDtypeStruct((8,) + weight.shape, weight.dtype),
        ),
        in_specs=[IN_VMEM] * 3,
        out_specs=(IN_VMEM,) * 3,
        scratch_shapes=[
            dma((9,)), dma((9,)), dma((7,)), dma((7,)), dma((8,)), dma((8,)),
            dma((7,)), dma((7,)), dma((2, 4)), dma((2, 4)), dma((8,)), dma((8,)), dma((3,)),
        ],
        compiler_params=params(1, vmem_limit_bytes=16 << 20),
        name="tp_gather",
    )(rows, seg, weight)


TILE = 128


def attention_kernel(
    kv_ref, q_ref, start_ref, tokens_ref, w_out_ref, gain_ref, router_ref, routes_ref,
    resid_ref, payload_ref,
    slots, peak, total, mixed, heads_out, heads_in,
    z_send, z_recv, y_send, y_recv, c_send, c_recv,
    h_send, h_recv, local,
):
    s, t, _, _, core, x, y = places()
    own = x * 4
    up, down, two = (y + 1) % 4, (y + 3) % 4, (y + 2) % 4
    far = ((s + 4) % 32, t)
    near = ((s + 2) % 32, t)
    yn, yp = (s, own + up), (s, own + down)
    twin = (s + 1 - 2 * core, t)
    tp_peers = [(s, (t + k) % 8) for k in range(1, 8)]
    greet(tp_peers + [twin, near, far, ((s + 30) % 32, t), ((s + 28) % 32, t)])
    moves = Copies(twin)
    count = q_ref.shape[0]

    kv_own = pltpu.make_async_copy(kv_ref, slots.at[0], local.at[0])
    kv_own.start()
    moves.start(kv_ref.at[y], slots.at[2, y], z_send.at[0], z_recv.at[0], near)
    moves.start(kv_ref.at[y], slots.at[4, y], z_send.at[1], z_recv.at[1], far)
    peak[...] = jnp.full_like(peak, NEGATIVE)
    total[...] = jnp.zeros_like(total)
    mixed[...] = jnp.zeros_like(mixed)
    base = s * count
    unit = math.log2(math.e) / math.sqrt(HD)

    def attend(j):
        def tile(number, _):
            rows = pl.ds(pl.multiple_of(number * TILE, TILE), TILE)
            keys = slots[j, :, 0].reshape(count, HD)
            values = slots[j, :, 1].reshape(count, HD)
            scores = lax.dot_general(
                q_ref[rows, :], keys, (((1,), (1,)), ((), ())), preferred_element_type=jnp.float32
            ) * unit
            key_index = base - j * count + lax.broadcasted_iota(jnp.int32, (1, count), 1)
            allowed = key_index >= start_ref[rows, :]
            if j == 0:
                query_index = base + number * TILE + lax.broadcasted_iota(jnp.int32, (TILE, 1), 0)
                allowed = allowed & (key_index <= query_index)
            masked = jnp.where(allowed, scores, NEGATIVE)
            old = peak[rows, :]
            newest = jnp.maximum(old, jnp.max(masked, axis=-1, keepdims=True))
            factor = jnp.exp2(old - newest)
            weights = jnp.exp2(masked - newest)
            total[rows, :] = total[rows, :] * factor + jnp.sum(weights, axis=-1, keepdims=True)
            mixed[rows, :] = mixed[rows, :] * factor + jnp.dot(
                weights.astype(jnp.bfloat16), values, preferred_element_type=jnp.float32
            )
            peak[rows, :] = newest
            return 0

        lax.fori_loop(0, count // TILE, tile, 0)

    def z_step(k, onward):
        piece = slots.at[2 * k, y]
        moves.landed(piece, z_send.at[k - 1], z_recv.at[k - 1])
        if onward:
            moves.start(piece, slots.at[2 * k + 4, y], z_send.at[k + 1], z_recv.at[k + 1], far)
        moves.start(piece, piece, y_send.at[k - 1, 0], y_recv.at[k - 1, 0], yn)
        moves.start(piece, piece, y_send.at[k - 1, 1], y_recv.at[k - 1, 1], yp)

    def y_step(k):
        moves.landed(slots.at[2 * k, down], y_send.at[k - 1, 0], y_recv.at[k - 1, 0])
        piece = slots.at[2 * k, down, 0]
        moves.start(piece, piece, y_send.at[k - 1, 2], y_recv.at[k - 1, 2], yn)
        moves.landed(slots.at[2 * k, up], y_send.at[k - 1, 1], y_recv.at[k - 1, 1])
        piece = slots.at[2 * k, up, 1]
        moves.start(piece, piece, y_send.at[k - 1, 3], y_recv.at[k - 1, 3], yp)

    def block_step(k):
        moves.landed(slots.at[2 * k, two, 0], y_send.at[k - 1, 2], y_recv.at[k - 1, 2])
        moves.landed(slots.at[2 * k, two, 1], y_send.at[k - 1, 3], y_recv.at[k - 1, 3])
        moves.start(
            slots.at[2 * k - 2 + 2 * core], slots.at[2 * k - 1], c_send.at[k - 1], c_recv.at[k - 1], twin
        )

    def twin_step(k):
        moves.landed(slots.at[2 * k - 1], c_send.at[k - 1], c_recv.at[k - 1])
        attend(2 * k - 1)

    kv_own.wait()
    attend(0)
    z_step(1, True)
    z_step(2, True)
    y_step(1)
    y_step(2)
    block_step(1)
    block_step(2)
    attend(2)
    z_step(3, False)
    z_step(4, False)
    twin_step(1)
    y_step(3)
    y_step(4)
    attend(4)
    block_step(3)
    block_step(4)
    twin_step(2)
    attend(6)
    twin_step(3)
    attend(8)
    twin_step(4)

    for rank in range(8):
        rows = pl.ds(rank * 64, 64)
        heads_out[rank] = (mixed[rows, :] / total[rows, :]).astype(heads_out.dtype)
    heads_own = pltpu.make_async_copy(heads_out.at[t], heads_in.at[t], local.at[0])
    heads_own.start()
    for k, peer in enumerate(tp_peers):
        moves.start(heads_out.at[peer[1]], heads_in.at[t], h_send.at[k], h_recv.at[k], peer)
    heads_own.wait()
    for k in range(7):
        moves.landed(heads_in.at[t], h_send.at[k], h_recv.at[k])
    attention = jnp.concatenate([heads_in[rank] for rank in range(8)], axis=1)
    width = tokens_ref.shape[1]
    resid = tokens_ref[...].astype(jnp.float32) + jnp.dot(
        attention, w_out_ref[...], preferred_element_type=jnp.float32
    )
    resid_ref[...] = resid
    moe_rows = rms_rows(resid, gain_ref[...]).astype(jnp.bfloat16)
    payload_ref[:, :width] = moe_rows
    logits = jnp.dot(moe_rows, router_ref[...], preferred_element_type=jnp.float32)
    experts = logits.shape[1]
    expert_ids = lax.broadcasted_iota(jnp.int32, logits.shape, 1)
    routes = routes_ref[...]
    picked = [routes[:, k : k + 1] == expert_ids for k in range(routes.shape[1])]
    chosen = [jnp.sum(jnp.where(one, logits, 0.0), axis=1, keepdims=True) for one in picked]
    highest = functools.reduce(jnp.maximum, chosen)
    powers = [jnp.exp(one - highest) for one in chosen]
    whole = functools.reduce(jnp.add, powers)
    table = jnp.zeros_like(logits)
    for one, power in zip(picked, powers):
        table = jnp.where(one, power / whole, table)
    payload_ref[:, width:] = jnp.zeros((logits.shape[0], HD), jnp.bfloat16)
    payload_ref[:, width : width + experts] = table.astype(jnp.bfloat16)
    moves.drain()


def attention_layer(kv, query, starts, tokens, w_out, gain, router, routes):
    dma = pltpu.SemaphoreType.DMA
    bf16, f32 = jnp.bfloat16, jnp.float32
    rows, width = tokens.shape
    count = query.shape[0]
    return pl.pallas_call(
        attention_kernel,
        out_shape=(
            jax.ShapeDtypeStruct((rows, width), f32),
            jax.ShapeDtypeStruct((rows, width + HD), bf16),
        ),
        in_specs=[IN_VMEM] * 8,
        out_specs=(IN_VMEM,) * 2,
        scratch_shapes=[
            pltpu.VMEM((9,) + kv.shape, bf16),
            pltpu.VMEM((count, 1), f32),
            pltpu.VMEM((count, 1), f32),
            pltpu.VMEM((count, HD), f32),
            pltpu.VMEM((8, rows, HD), bf16),
            pltpu.VMEM((8, rows, HD), bf16),
            dma((4,)), dma((4,)), dma((4, 4)), dma((4, 4)), dma((4,)), dma((4,)),
            dma((7,)), dma((7,)), dma((1,)),
        ],
        compiler_params=params(2, vmem_limit_bytes=20 << 20),
        name="attention_layer",
    )(kv, query, starts, tokens, w_out, gain, router, routes)


HALF = 32


def ring_places():
    s, t, plane, z, core, x, y = places()
    across = ((1 - plane) * 16 + z * 2 + core, (1 - x) * 4 + y)
    twin = (s + 1 - 2 * core, t)
    ring = [(plane * 16 + ((z + d) % 8) * 2 + core, t) for d in (1, 7)]
    return s, z, core, [plane, 1 - plane], across, twin, ring


def spread_kernel(
    rows_ref, out_ref, ax_send, ax_recv, az_send, az_recv,
    bx_send, bx_recv, bz_send, bz_recv, c_send, c_recv, local,
):
    s, z, core, planes, across, twin, ring = ring_places()
    greet([across, twin] + ring)
    moves = Copies(twin)
    part_a, part_b = pl.ds(0, HALF), pl.ds(HALF, HALF)
    quarters = [pl.ds(HALF, HALF // 2), pl.ds(HALF + HALF // 2, HALF // 2)]

    def slot(p, way, distance):
        back = (z + 8 - distance) % 8 if way == 0 else (z + distance) % 8
        return planes[p] * 16 + back * 2 + core

    twins = []

    def to_twin(src, block, part):
        k = len(twins)
        twins.append(part)
        moves.start(src, out_ref.at[block, part], c_send.at[k], c_recv.at[k], twin)

    crossed = []

    def cross(src, block):
        k = len(crossed)
        crossed.append(k)
        moves.start(src, out_ref.at[block, part_b], bx_send.at[k], bx_recv.at[k], across)

    def a_travels(p, way, distance):
        return distance <= 3 or (distance == 4 and p == way)

    def a_arrives(p, way, distance):
        if not a_travels(p, way, distance):
            return
        block, k = slot(p, way, distance), distance - 1
        piece = out_ref.at[block, part_a]
        moves.landed(piece, az_send.at[p, way, k], az_recv.at[p, way, k])
        if a_travels(p, way, distance + 1):
            moves.start(piece, piece, az_send.at[p, way, k + 1], az_recv.at[p, way, k + 1], ring[way])
        to_twin(piece, block, part_a)

    def b_arrives(way, distance):
        block, k = slot(0, way, distance), distance - 1
        if distance == 4:
            piece = out_ref.at[block, quarters[way]]
            moves.landed(piece, bz_send.at[way, k], bz_recv.at[way, k])
            if way == 0:
                return
        piece = out_ref.at[block, part_b]
        if distance < 4:
            moves.landed(piece, bz_send.at[way, k], bz_recv.at[way, k])
            onward = out_ref.at[block, quarters[way]] if distance == 3 else piece
            moves.start(onward, onward, bz_send.at[way, k + 1], bz_recv.at[way, k + 1], ring[way])
        cross(piece, block)
        to_twin(piece, block, part_b)

    def b_crossed(k, way, distance):
        block = slot(1, way, distance)
        piece = out_ref.at[block, part_b]
        moves.landed(piece, bx_send.at[k], bx_recv.at[k])
        to_twin(piece, block, part_b)

    own = pltpu.make_async_copy(rows_ref, out_ref.at[s], local)
    own.start()
    own_a, own_b = rows_ref.at[part_a], rows_ref.at[part_b]
    moves.start(own_a, out_ref.at[s, part_a], ax_send, ax_recv, across)
    for way in range(2):
        moves.start(own_b, out_ref.at[s, part_b], bz_send.at[way, 0], bz_recv.at[way, 0], ring[way])
    for way in range(2):
        moves.start(own_a, out_ref.at[s, part_a], az_send.at[0, way, 0], az_recv.at[0, way, 0], ring[way])
    cross(own_b, s)
    to_twin(own_a, s, part_a)
    to_twin(own_b, s, part_b)
    block = across[0]
    piece = out_ref.at[block, part_a]
    moves.landed(piece, ax_send, ax_recv)
    for way in range(2):
        moves.start(piece, piece, az_send.at[1, way, 0], az_recv.at[1, way, 0], ring[way])
    to_twin(piece, block, part_a)
    for distance in range(1, 5):
        for way in range(2):
            b_arrives(way, distance)
        for p in range(2):
            for way in range(2):
                a_arrives(p, way, distance)
        if distance == 1:
            b_crossed(0, 0, 0)
        else:
            b_crossed(2 * distance - 3, 0, distance - 1)
            b_crossed(2 * distance - 2, 1, distance - 1)
    b_crossed(7, 0, 4)
    own.wait()
    for k, part in enumerate(twins):
        moves.landed(out_ref.at[twin[0], part], c_send.at[k], c_recv.at[k])
    moves.drain()


def spread(rows):
    dma = pltpu.SemaphoreType.DMA
    return pl.pallas_call(
        spread_kernel,
        out_shape=jax.ShapeDtypeStruct((32,) + rows.shape, rows.dtype),
        in_specs=[IN_VMEM],
        out_specs=IN_VMEM,
        scratch_shapes=[
            dma(()), dma(()), dma((2, 2, 4)), dma((2, 2, 4)), dma((8,)), dma((8,)),
            dma((2, 4)), dma((2, 4)), dma((32,)), dma((32,)), dma(()),
        ],
        compiler_params=params(4, vmem_limit_bytes=12 << 20),
        name="spread",
    )(rows)


CHUNK = 256


def expert_kernel(rows_ref, gate_ref, up_ref, down_ref, out_ref, column, lane, gathered, contribution, starts):
    width = gate_ref.shape[0]
    blocks = rows_ref.shape[0] // CHUNK
    expert = lax.axis_index("seq")
    bf16, f32 = jnp.bfloat16, jnp.float32
    down_index = lax.broadcasted_iota(jnp.int32, (CHUNK, CHUNK), 0)
    along_index = lax.broadcasted_iota(jnp.int32, (CHUNK, CHUNK), 1)
    zero_first = (((0,), (0,)), ((), ()))

    def span(block):
        return pl.ds(pl.multiple_of(block * CHUNK, CHUNK), CHUNK)

    def number_rows(block, before):
        routed = (rows_ref[span(block), width:].astype(f32) != 0.0).astype(f32)
        here = lax.broadcasted_iota(jnp.int32, routed.shape, 1) == expert
        routed = jnp.where(here, routed, 0.0)
        ones = routed.astype(bf16)
        upto = jnp.dot((along_index <= down_index).astype(f32).astype(bf16), ones, preferred_element_type=f32)
        hit = jnp.sum(routed, axis=1, keepdims=True)
        rank = jnp.sum(jnp.where(here, upto, 0.0), axis=1, keepdims=True)
        column[span(block), :] = jnp.where(hit > 0.0, rank + (before - 1.0), -1.0)
        upto = lax.dot_general(
            ones, (down_index <= along_index).astype(f32).astype(bf16), zero_first, preferred_element_type=f32
        )
        same = lax.dot_general(
            ones, (down_index == along_index).astype(f32).astype(bf16), zero_first, preferred_element_type=f32
        )
        hit = jnp.sum(same, axis=0, keepdims=True)
        mine = lax.broadcasted_iota(jnp.int32, upto.shape, 0) == expert
        rank = jnp.sum(jnp.where(mine, upto, 0.0), axis=0, keepdims=True)
        lane[block] = jnp.where(hit > 0.0, rank + (before - 1.0), -1.0)
        starts[block] = before.astype(jnp.int32)
        return before + jnp.sum(routed)

    routed = lax.fori_loop(0, blocks, number_rows, jnp.float32(0.0)).astype(jnp.int32)
    starts[blocks] = routed

    def one_chunk(number, _):
        base = number * CHUNK
        gathered[...] = jnp.zeros_like(gathered)

        def touches(block):
            first, end = starts[block], starts[block + 1]
            return (first < base + CHUNK) & ((end > base) | (first >= base))

        def gather(block, _):
            @pl.when(touches(block))
            def _():
                slots = base + lax.broadcasted_iota(jnp.int32, (CHUNK, 1), 0)
                picks = (lane[block] == slots.astype(f32)).astype(f32).astype(bf16)
                gathered[...] += jnp.dot(picks, rows_ref[span(block), :], preferred_element_type=f32)

            return 0

        lax.fori_loop(0, blocks, gather, 0)
        all_gates = gathered[:, width:]
        here = lax.broadcasted_iota(jnp.int32, all_gates.shape, 1) == expert
        gates = jnp.sum(jnp.where(here, all_gates, 0.0), axis=1, keepdims=True)
        rows = gathered[:, :width].astype(bf16)
        gate_out = jnp.dot(rows, gate_ref[...], preferred_element_type=f32)
        up_out = jnp.dot(rows, up_ref[...], preferred_element_type=f32)
        active = (jnp.maximum(gate_out, 0.0) * up_out).astype(bf16)
        down_out = jnp.dot(active, down_ref[...], preferred_element_type=f32) * gates
        contribution[...] = down_out.astype(bf16)

        def place(block, _):
            @pl.when(touches(block))
            def _():
                slots = base + lax.broadcasted_iota(jnp.int32, (1, CHUNK), 1)
                back = (column[span(block), :] == slots.astype(f32)).astype(f32).astype(bf16)
                placed = jnp.dot(back, contribution[...], preferred_element_type=f32)

                @pl.when(starts[block] >= base)
                def _():
                    out_ref[span(block), :] = placed.astype(bf16)

                @pl.when(starts[block] < base)
                def _():
                    out_ref[span(block), :] = (out_ref[span(block), :].astype(f32) + placed).astype(bf16)

            return 0

        lax.fori_loop(0, blocks, place, 0)
        return 0

    lax.fori_loop(0, routed // CHUNK + 1, one_chunk, 0)


def run_expert(rows, w_gate, w_up, w_down):
    tokens, columns = rows.shape
    width = w_gate.shape[0]
    return pl.pallas_call(
        expert_kernel,
        out_shape=jax.ShapeDtypeStruct((tokens, width), jnp.bfloat16),
        in_specs=[IN_VMEM] * 4,
        out_specs=IN_VMEM,
        scratch_shapes=[
            pltpu.VMEM((tokens, 1), jnp.float32),
            pltpu.VMEM((tokens // CHUNK, 1, CHUNK), jnp.float32),
            pltpu.VMEM((CHUNK, columns), jnp.float32),
            pltpu.VMEM((CHUNK, width), jnp.bfloat16),
            pltpu.SMEM((tokens // CHUNK + 1,), jnp.int32),
        ],
        compiler_params=pltpu.CompilerParams(vmem_limit_bytes=28 << 20),
        name="run_expert",
    )(rows, w_gate, w_up, w_down)


def collect_kernel(
    in_ref, out_ref, other, total_a, total_b, a_in, b_in, bx_in, from_x,
    ax_send, ax_recv, az_send, az_recv, bx_send, bx_recv, bz_send, bz_recv, c_send, c_recv,
):
    s, z, core, planes, across, twin, ring = ring_places()
    greet([across, twin] + ring)
    moves = Copies(twin)
    part_a, part_b = pl.ds(0, HALF), pl.ds(HALF, HALF)
    quarters = [pl.ds(0, HALF // 2), pl.ds(HALF // 2, HALF // 2)]
    wide = lambda values: values.astype(jnp.float32)

    def place(p, way, distance):
        ahead = (z + distance) % 8 if way == 0 else (z + 8 - distance) % 8
        return ahead, planes[p] * 8 + ahead

    order = [(1, 0, 4), (0, 0, 4)]
    for distance in (3, 2, 1):
        order += [(p, way, distance) for p in (1, 0) for way in range(2)]
    order += [(1, 0, 0), (0, 0, 0)]
    for k, key in enumerate(order):
        _, i = place(*key)
        moves.start(in_ref.at[2 * i + 1 - core], other.at[i], c_send.at[k], c_recv.at[k], twin)

    crossed = {}
    for k, (p, way, distance) in enumerate(order):
        ahead, i = place(p, way, distance)
        moves.landed(other.at[i], c_send.at[k], c_recv.at[k])

        mine = wide(in_ref[2 * i + core, part_b]) + wide(other[i, part_b])
        if p == 1:
            total_b[i] = mine.astype(jnp.bfloat16)
            j = len(crossed)
            crossed[way, distance] = j
            moves.start(total_b.at[i], bx_in.at[ahead], bx_send.at[j], bx_recv.at[j], across)

        ours = wide(in_ref[2 * i + core, part_a]) + wide(other[i, part_a])
        if distance > 0:
            ways = [p] if distance == 4 else [way]
            for w in ways:
                if distance < (4 if p == w else 3):
                    piece = a_in.at[p, w, distance]
                    moves.landed(piece, az_send.at[p, w, distance], az_recv.at[p, w, distance])
                    ours = ours + wide(piece[...])
                total_a[i] = ours.astype(jnp.bfloat16)
                moves.start(
                    total_a.at[i], a_in.at[p, w, distance - 1],
                    az_send.at[p, w, distance - 1], az_recv.at[p, w, distance - 1], ring[w],
                )
        else:
            for w in range(2):
                piece = a_in.at[p, w, 0]
                moves.landed(piece, az_send.at[p, w, 0], az_recv.at[p, w, 0])
                ours = ours + wide(piece[...])
            if p == 1:
                total_a[i] = ours.astype(jnp.bfloat16)
                moves.start(total_a.at[i], from_x, ax_send, ax_recv, across)

        if p == 0:
            j = crossed[way, distance]
            moves.landed(bx_in.at[ahead], bx_send.at[j], bx_recv.at[j])
            mine = mine + wide(bx_in[ahead])
            if distance == 4:
                total_b[i] = mine.astype(jnp.bfloat16)
                for w in range(2):
                    moves.start(
                        total_b.at[i, quarters[w]], b_in.at[w, 3, quarters[w]],
                        bz_send.at[w, 3], bz_recv.at[w, 3], ring[w],
                    )
            elif distance == 3:
                piece = b_in.at[way, 3, quarters[way]]
                moves.landed(piece, bz_send.at[way, 3], bz_recv.at[way, 3])
                split = HALF // 2
                first, second = mine[:split], mine[split:]
                if way == 0:
                    first = first + wide(piece[...])
                else:
                    second = second + wide(piece[...])
                total_b[i, quarters[0]] = first.astype(jnp.bfloat16)
                total_b[i, quarters[1]] = second.astype(jnp.bfloat16)
            elif distance > 0:
                piece = b_in.at[way, distance]
                moves.landed(piece, bz_send.at[way, distance], bz_recv.at[way, distance])
                total_b[i] = (mine + wide(piece[...])).astype(jnp.bfloat16)
            if 0 < distance < 4:
                moves.start(
                    total_b.at[i], b_in.at[way, distance - 1],
                    bz_send.at[way, distance - 1], bz_recv.at[way, distance - 1], ring[way],
                )
            if distance == 0:
                for w in range(2):
                    piece = b_in.at[w, 0]
                    moves.landed(piece, bz_send.at[w, 0], bz_recv.at[w, 0])
                    mine = mine + wide(piece[...])
                out_ref[part_b, :] = mine.astype(out_ref.dtype)
                moves.landed(from_x, ax_send, ax_recv)
                out_ref[part_a, :] = (ours + wide(from_x[...])).astype(out_ref.dtype)
    moves.drain()


def collect(parts):
    dma = pltpu.SemaphoreType.DMA
    _, rows, width = parts.shape
    vmem = lambda *lead: pltpu.VMEM(lead + (width,), parts.dtype)
    return pl.pallas_call(
        collect_kernel,
        out_shape=jax.ShapeDtypeStruct((rows, width), jnp.bfloat16),
        in_specs=[IN_VMEM],
        out_specs=IN_VMEM,
        scratch_shapes=[
            vmem(16, rows), vmem(16, HALF), vmem(16, HALF), vmem(2, 2, 4, HALF), vmem(2, 4, HALF),
            vmem(8, HALF), vmem(HALF),
            dma(()), dma(()), dma((2, 2, 4)), dma((2, 2, 4)), dma((8,)), dma((8,)),
            dma((2, 4)), dma((2, 4)), dma((16,)), dma((16,)),
        ],
        compiler_params=params(5, vmem_limit_bytes=28 << 20),
        name="collect",
    )(parts)


def on_device(
    tokens, segment_ids, routes, attn_gain, w_query, w_key, w_value, w_out,
    moe_gain, w_router, w_gate, w_up, w_down,
):
    tp_rank = lax.axis_index("tp")
    seq_rank = lax.axis_index("seq")
    tok_dev, width = tokens.shape
    tok_seq = tok_dev * 8
    bf16, f32 = jnp.bfloat16, jnp.float32
    block_first = seq_rank * tok_seq

    seg_row = jnp.pad(segment_ids, (0, HD - tok_dev), constant_values=-1).reshape(1, HD)
    wide, segs, w_out_all = tp_gather(tokens, seg_row, w_out.reshape(16, 8, width))

    block_index = block_first + jnp.arange(tok_seq, dtype=jnp.int32)
    near = segs[:, :, 0, :tok_dev].reshape(9, tok_seq)
    near_index = block_index[None, :] - tok_seq * jnp.arange(9, dtype=jnp.int32)[:, None]
    labels = jnp.arange(6, dtype=jnp.int32)
    hits = (near[None] == labels[:, None, None]) & (near_index >= 0)[None]
    firsts = jnp.min(jnp.where(hits, near_index[None], 1 << 30), axis=(1, 2))
    starts = jnp.sum(jnp.where(near[0][:, None] == labels[None, :], firsts[None, :], 0), axis=1)
    position = (block_index - starts).astype(f32)
    inverse = ROTARY ** (-(jnp.arange(HD // 2, dtype=f32) * 2.0 / HD))
    angle = position[:, None] * inverse[None, :]
    cosine, sine = jnp.cos(angle), jnp.sin(angle)

    normed = rms_rows(wide.reshape(tok_seq, width), attn_gain).astype(bf16)
    query = rotate(jnp.dot(normed, w_query, preferred_element_type=f32), cosine, sine).astype(bf16)
    keys = rotate(jnp.dot(normed, w_key, preferred_element_type=f32), cosine, sine).astype(bf16)
    values = jnp.dot(normed, w_value, preferred_element_type=f32).astype(bf16)

    def own_rows(matrix):
        mine = lax.dynamic_slice_in_dim(matrix, tp_rank * tok_dev, tok_dev, 0)
        return jnp.transpose(mine.reshape(tok_dev, KVH, HD), (1, 0, 2))

    kv_cache = jnp.stack([own_rows(keys), own_rows(values)])
    head = tp_rank // 4
    kv_own = jnp.stack(
        [
            lax.dynamic_slice_in_dim(m, head * HD, HD, 1).reshape(4, tok_seq // 4, HD)
            for m in (keys, values)
        ],
        axis=1,
    )
    resid, payload = attention_layer(
        kv_own, query, starts[:, None], tokens, w_out_all.reshape(QH * HD, width), moe_gain[None], w_router, routes
    )
    arrived = spread(payload).reshape(32 * tok_dev, width + HD)
    parts = run_expert(arrived, w_gate[0], w_up[0], w_down[0])
    moe = collect(parts.reshape(32, tok_dev, width))
    layer_out = (resid + moe.astype(f32)).astype(bf16)
    return (layer_out, kv_cache)


def solution(mesh):
    placed = (
        P(("seq", "tp"), None),
        P(("seq", "tp")),
        P(("seq", "tp"), None),
        P(),
        P(None, "tp"),
        P(),
        P(),
        P("tp", None),
        P(),
        P(),
        P("seq", None, None),
        P("seq", None, None),
        P("seq", None, None),
    )
    return jax.shard_map(
        on_device,
        mesh=mesh,
        in_specs=placed,
        out_specs=(P(("seq", "tp"), None), P(None, None, ("seq", "tp"), None)),
        check_vma=False,
    )
```

```python
import functools
import math

import jax
import jax.numpy as jnp
from jax import lax
from jax.experimental import pallas as pl
from jax.experimental.pallas import tpu as pltpu
from jax.sharding import PartitionSpec as P

HD = 128
QH = 8
KVH = 2
ROTARY = 1000000.0
NEGATIVE = -1e30
MESH = pl.DeviceIdType.MESH
ANY = pl.BlockSpec(memory_space=pl.ANY)
IN_VMEM = pl.BlockSpec(memory_space=pltpu.VMEM)


def rms_rows(values_in, gain):
    wide = values_in.astype(jnp.float32)
    scale = lax.rsqrt(jnp.mean(wide * wide, axis=-1, keepdims=True) + 1e-06)
    return wide * scale * gain


def rotate(matrix, cosine, sine):
    count = matrix.shape[0]
    shaped = matrix.reshape(count, -1, HD)
    half = HD // 2
    cosine, sine = cosine[:, None, :], sine[:, None, :]
    first = shaped[..., :half]
    second = shaped[..., half:]
    turned = jnp.concatenate(
        [first * cosine - second * sine, second * cosine + first * sine], axis=-1
    )
    return turned.reshape(count, -1)


def greet(peers):
    barrier = pltpu.get_barrier_semaphore()
    for peer in peers:
        pl.semaphore_signal(barrier, inc=1, device_id=peer, device_id_type=MESH)
    pl.semaphore_wait(barrier, len(peers))


def places():
    s, t = lax.axis_index("seq"), lax.axis_index("tp")
    return s, t, s // 16, (s // 2) % 8, s % 2, t // 4, t % 4


def params(number, **more):
    return pltpu.CompilerParams(collective_id=number, has_side_effects=True, **more)


class Copies:
    def __init__(self, anyone):
        self.anyone, self.sent = anyone, []

    def start(self, src, dst, send, recv, peer):
        copy = pltpu.make_async_remote_copy(
            src_ref=src, dst_ref=dst, send_sem=send, recv_sem=recv,
            device_id=peer, device_id_type=MESH,
        )
        copy.start()
        self.sent.append(copy)

    def landed(self, dst, send, recv):
        pltpu.make_async_remote_copy(
            src_ref=dst, dst_ref=dst, send_sem=send, recv_sem=recv,
            device_id=self.anyone, device_id_type=MESH,
        ).wait_recv()

    def drain(self):
        for copy in self.sent:
            copy.wait_send()


def tp_gather_kernel(
    rows_ref, seg_ref, gain_ref, w_query_ref, w_key_ref, w_value_ref,
    query_ref, key_ref, value_ref, own_key_ref, own_value_ref, segs_ref,
    out, w_query, w_key_value,
    send, recv, seg_send, seg_recv, far_send, far_recv, local,
):
    s, t, _, _, core, x, y = places()
    across = (1 - x) * 4
    own = x * 4
    up, down, two = (y + 1) % 4, (y + 3) % 4, (y + 2) % 4
    xp, yn, yp = (s, across + y), (s, own + up), (s, own + down)
    tp_peers = [(s, (t + k) % 8) for k in range(1, 8)]
    ahead = [((s + k) % 32, t) for k in range(1, 9)]
    behind = [((s + 32 - k) % 32, t) for k in range(1, 9)]
    greet(tp_peers + ahead + behind)
    moves = Copies(xp)

    def go(number, src, dst, peer):
        moves.start(src, dst, send.at[number], recv.at[number], peer)

    def landed(number, dst):
        moves.landed(dst, send.at[number], recv.at[number])

    seg_own = pltpu.make_async_copy(seg_ref, segs_ref.at[0, t], local.at[0])
    seg_own.start()
    for k, peer in enumerate(tp_peers):
        moves.start(seg_ref, segs_ref.at[0, t], seg_send.at[k], seg_recv.at[k], peer)
    go(0, rows_ref, out.at[t], xp)
    go(1, rows_ref, out.at[t], yn)
    go(2, rows_ref, out.at[t], yp)
    rows_own = pltpu.make_async_copy(rows_ref, out.at[t], local.at[1])
    rows_own.start()
    columns = w_key_ref.shape[1]
    loads = [
        pltpu.make_async_copy(w_query_ref, w_query, local.at[2]),
        pltpu.make_async_copy(w_key_ref, w_key_value.at[:, pl.ds(0, columns)], local.at[3]),
        pltpu.make_async_copy(w_value_ref, w_key_value.at[:, pl.ds(columns, columns)], local.at[4]),
    ]
    for load in loads:
        load.start()

    def normed(rank):
        return rms_rows(out[rank], gain_ref[...]).astype(jnp.bfloat16)

    def project(rank):
        rows = normed(rank)
        span = pl.ds(pl.multiple_of(rank * rows.shape[0], 64), rows.shape[0])
        query_ref[span, :] = jnp.dot(rows, w_query[...], preferred_element_type=jnp.float32)
        for offset, target in ((0, key_ref), (columns, value_ref)):
            head = pl.ds(pl.multiple_of(offset + x * HD, HD), HD)
            target[span, :] = jnp.dot(
                rows, w_key_value[:, head], preferred_element_type=jnp.float32
            ).astype(target.dtype)

    seg_own.wait()
    for k in range(7):
        moves.landed(segs_ref.at[0, t], seg_send.at[k], seg_recv.at[k])
    for k, peer in enumerate(ahead):
        moves.start(segs_ref.at[0], segs_ref.at[k + 1], far_send.at[k], far_recv.at[k], peer)
    low, high = pl.ds(0, 32), pl.ds(32, 32)
    rows_own.wait()
    for load in loads:
        load.wait()
    both = jnp.dot(normed(t), w_key_value[...], preferred_element_type=jnp.float32)
    own_key_ref[...] = both[:, :columns]
    own_value_ref[...] = both[:, columns:].astype(jnp.bfloat16)
    project(t)
    landed(0, out.at[across + y])
    go(3, out.at[across + y], out.at[across + y], yn)
    go(4, out.at[across + y], out.at[across + y], yp)
    landed(1, out.at[own + down])
    go(5, out.at[own + down, low], out.at[own + down, low], yn)
    landed(2, out.at[own + up])
    go(6, out.at[own + up, high], out.at[own + up, high], yp)
    project(across + y)
    landed(3, out.at[across + down])
    go(7, out.at[across + down, low], out.at[across + down, low], yn)
    landed(4, out.at[across + up])
    go(8, out.at[across + up, high], out.at[across + up, high], yp)
    project(own + down)
    project(own + up)
    project(across + down)
    project(across + up)
    landed(5, out.at[own + two, low])
    landed(6, out.at[own + two, high])
    project(own + two)
    landed(7, out.at[across + two, low])
    landed(8, out.at[across + two, high])
    project(across + two)
    for k in range(8):
        moves.landed(segs_ref.at[k + 1], far_send.at[k], far_recv.at[k])
    moves.drain()


def tp_gather(rows, seg, gain, w_query, w_key, w_value):
    count, width = rows.shape
    dma = pltpu.SemaphoreType.DMA
    bf16, f32 = jnp.bfloat16, jnp.float32
    shape = jax.ShapeDtypeStruct
    return pl.pallas_call(
        tp_gather_kernel,
        out_shape=(
            shape((8 * count, HD), f32),
            shape((8 * count, HD), f32),
            shape((8 * count, HD), bf16),
            shape((count, KVH * HD), f32),
            shape((count, KVH * HD), bf16),
            shape((9, 8, 1, 128), jnp.int32),
        ),
        in_specs=[IN_VMEM] * 3 + [ANY] * 3,
        out_specs=(IN_VMEM,) * 6,
        scratch_shapes=[
            pltpu.VMEM((8, count, width), bf16),
            pltpu.VMEM((width, HD), bf16),
            pltpu.VMEM((width, 2 * KVH * HD), bf16),
            dma((9,)), dma((9,)), dma((7,)), dma((7,)), dma((8,)), dma((8,)), dma((5,)),
        ],
        compiler_params=params(1, vmem_limit_bytes=20 << 20),
        name="tp_gather",
    )(rows, seg, gain, w_query, w_key, w_value)


TILE = 256


def attention_kernel(
    kv_ref, q_ref, start_ref, tokens_ref, w_out_ref, gain_ref, router_ref, routes_ref,
    resid_ref, payload_ref,
    slots, w_full, peak, total, mixed, heads_out, heads_in,
    z_send, z_recv, y_send, y_recv, c_send, c_recv,
    w_send, w_recv, t_send, t_recv, h_send, h_recv, local,
):
    s, t, _, _, core, x, y = places()
    across, own = (1 - x) * 4, x * 4
    up, down, two = (y + 1) % 4, (y + 3) % 4, (y + 2) % 4
    far = ((s + 4) % 32, t)
    near = ((s + 2) % 32, t)
    xp, yn, yp = (s, across + y), (s, own + up), (s, own + down)
    twin = (s + 1 - 2 * core, t)
    tp_peers = [(s, (t + k) % 8) for k in range(1, 8)]
    greet(tp_peers + [twin, near, far, ((s + 30) % 32, t), ((s + 28) % 32, t)])
    moves = Copies(twin)
    count = q_ref.shape[0]

    def w_piece(rank, half, first=0, rows=64):
        return w_full.at[rank, pl.ds(pl.multiple_of(half * 64 + first, 32), rows)]

    def w_go(number, rank, peer, first=0, rows=64):
        piece = w_piece(rank, core, first, rows)
        moves.start(piece, piece, w_send.at[number], w_recv.at[number], peer)

    def w_landed(number, rank, first=0, rows=64):
        moves.landed(w_piece(rank, core, first, rows), w_send.at[number], w_recv.at[number])

    def w_twin(number, rank):
        piece = w_piece(rank, core)
        moves.start(piece, piece, t_send.at[number], t_recv.at[number], twin)

    kv_own = pltpu.make_async_copy(kv_ref, slots.at[0], local.at[0])
    kv_own.start()
    w_own = pltpu.make_async_copy(w_out_ref, w_full.at[t], local.at[1])
    w_own.start()
    moves.start(kv_ref.at[y], slots.at[2, y], z_send.at[0], z_recv.at[0], near)
    moves.start(kv_ref.at[y], slots.at[4, y], z_send.at[1], z_recv.at[1], far)
    w_own.wait()
    w_go(0, t, xp)
    w_go(1, t, yn)
    w_go(2, t, yp)

    peak[...] = jnp.full_like(peak, NEGATIVE)
    total[...] = jnp.zeros_like(total)
    mixed[...] = jnp.zeros_like(mixed)
    base = s * count
    unit = math.log2(math.e) / math.sqrt(HD)

    def attend(j):
        def tile(number):
            rows = pl.ds(number * TILE, TILE)
            keys = slots[j, :, 0].reshape(count, HD)
            values = slots[j, :, 1].reshape(count, HD)
            scores = lax.dot_general(
                q_ref[rows, :], keys, (((1,), (1,)), ((), ())), preferred_element_type=jnp.float32
            ) * unit
            key_index = base - j * count + lax.broadcasted_iota(jnp.int32, (1, count), 1)
            allowed = key_index >= start_ref[rows, :]
            if j == 0:
                query_index = base + number * TILE + lax.broadcasted_iota(jnp.int32, (TILE, 1), 0)
                allowed = allowed & (key_index <= query_index)
            masked = jnp.where(allowed, scores, NEGATIVE)
            old = peak[rows, :]
            newest = jnp.maximum(old, jnp.max(masked, axis=-1, keepdims=True))
            factor = jnp.exp2(old - newest)
            weights = jnp.exp2(masked - newest)
            total[rows, :] = total[rows, :] * factor + jnp.sum(weights, axis=-1, keepdims=True)
            mixed[rows, :] = mixed[rows, :] * factor + jnp.dot(
                weights.astype(jnp.bfloat16), values, preferred_element_type=jnp.float32
            )
            peak[rows, :] = newest

        for number in range(count // TILE):
            tile(number)

    def z_step(k, onward):
        piece = slots.at[2 * k, y]
        moves.landed(piece, z_send.at[k - 1], z_recv.at[k - 1])
        if onward:
            moves.start(piece, slots.at[2 * k + 4, y], z_send.at[k + 1], z_recv.at[k + 1], far)
        moves.start(piece, piece, y_send.at[k - 1, 0], y_recv.at[k - 1, 0], yn)
        moves.start(piece, piece, y_send.at[k - 1, 1], y_recv.at[k - 1, 1], yp)

    def y_step(k):
        moves.landed(slots.at[2 * k, down], y_send.at[k - 1, 0], y_recv.at[k - 1, 0])
        piece = slots.at[2 * k, down, 0]
        moves.start(piece, piece, y_send.at[k - 1, 2], y_recv.at[k - 1, 2], yn)
        moves.landed(slots.at[2 * k, up], y_send.at[k - 1, 1], y_recv.at[k - 1, 1])
        piece = slots.at[2 * k, up, 1]
        moves.start(piece, piece, y_send.at[k - 1, 3], y_recv.at[k - 1, 3], yp)

    def block_step(k):
        moves.landed(slots.at[2 * k, two, 0], y_send.at[k - 1, 2], y_recv.at[k - 1, 2])
        moves.landed(slots.at[2 * k, two, 1], y_send.at[k - 1, 3], y_recv.at[k - 1, 3])
        moves.start(
            slots.at[2 * k - 2 + 2 * core], slots.at[2 * k - 1], c_send.at[k - 1], c_recv.at[k - 1], twin
        )

    def twin_step(k):
        moves.landed(slots.at[2 * k - 1], c_send.at[k - 1], c_recv.at[k - 1])
        attend(2 * k - 1)

    kv_own.wait()
    attend(0)
    z_step(1, True)
    z_step(2, True)
    w_landed(0, across + y)
    w_go(3, across + y, yn)
    w_go(4, across + y, yp)
    w_twin(0, across + y)
    y_step(1)
    y_step(2)
    w_landed(1, own + down)
    w_go(5, own + down, yn, 0, 32)
    w_twin(1, own + down)
    w_landed(2, own + up)
    w_go(6, own + up, yp, 32, 32)
    w_twin(2, own + up)
    block_step(1)
    attend(2)
    z_step(3, False)
    z_step(4, False)
    block_step(2)
    twin_step(1)
    y_step(3)
    y_step(4)
    attend(4)
    w_landed(3, across + down)
    w_go(7, across + down, yn, 0, 32)
    w_twin(3, across + down)
    w_landed(4, across + up)
    w_go(8, across + up, yp, 32, 32)
    w_twin(4, across + up)
    block_step(3)
    twin_step(2)
    block_step(4)
    attend(6)
    twin_step(3)
    w_landed(5, own + two, 0, 32)
    w_landed(6, own + two, 32, 32)
    w_twin(5, own + two)
    attend(8)
    w_landed(7, across + two, 0, 32)
    w_landed(8, across + two, 32, 32)
    w_twin(6, across + two)
    twin_step(4)

    for rank in range(8):
        rows = pl.ds(rank * 64, 64)
        heads_out[rank] = (mixed[rows, :] / total[rows, :]).astype(heads_out.dtype)
    heads_own = pltpu.make_async_copy(heads_out.at[t], heads_in.at[t], local.at[0])
    heads_own.start()
    for k, peer in enumerate(tp_peers):
        moves.start(heads_out.at[peer[1]], heads_in.at[t], h_send.at[k], h_recv.at[k], peer)
    ranks = [across + y, own + down, own + up, across + down, across + up, own + two, across + two]
    for number, rank in enumerate(ranks):
        moves.landed(w_piece(rank, 1 - core), t_send.at[number], t_recv.at[number])
    heads_own.wait()
    for k in range(7):
        moves.landed(heads_in.at[t], h_send.at[k], h_recv.at[k])
    attention = jnp.concatenate([heads_in[rank] for rank in range(8)], axis=1)
    width = tokens_ref.shape[1]
    resid = tokens_ref[...].astype(jnp.float32) + jnp.dot(
        attention, w_full[...].reshape(8 * HD, width), preferred_element_type=jnp.float32
    )
    resid_ref[...] = resid
    moe_rows = rms_rows(resid, gain_ref[...]).astype(jnp.bfloat16)
    payload_ref[:, :width] = moe_rows
    logits = jnp.dot(moe_rows, router_ref[...], preferred_element_type=jnp.float32)
    experts = logits.shape[1]
    expert_ids = lax.broadcasted_iota(jnp.int32, logits.shape, 1)
    routes = routes_ref[...]
    picked = [routes[:, k : k + 1] == expert_ids for k in range(routes.shape[1])]
    chosen = [jnp.sum(jnp.where(one, logits, 0.0), axis=1, keepdims=True) for one in picked]
    highest = functools.reduce(jnp.maximum, chosen)
    powers = [jnp.exp(one - highest) for one in chosen]
    whole = functools.reduce(jnp.add, powers)
    table = jnp.zeros_like(logits)
    for one, power in zip(picked, powers):
        table = jnp.where(one, power / whole, table)
    payload_ref[:, width:] = jnp.zeros((logits.shape[0], HD), jnp.bfloat16)
    payload_ref[:, width : width + experts] = table.astype(jnp.bfloat16)
    moves.drain()


def attention_layer(kv, query, starts, tokens, w_out, gain, router, routes):
    dma = pltpu.SemaphoreType.DMA
    bf16, f32 = jnp.bfloat16, jnp.float32
    rows, width = tokens.shape
    count = query.shape[0]
    return pl.pallas_call(
        attention_kernel,
        out_shape=(
            jax.ShapeDtypeStruct((rows, width), f32),
            jax.ShapeDtypeStruct((rows, width + HD), bf16),
        ),
        in_specs=[IN_VMEM] * 8,
        out_specs=(IN_VMEM,) * 2,
        scratch_shapes=[
            pltpu.VMEM((9,) + kv.shape, bf16),
            pltpu.VMEM((8, HD, width), bf16),
            pltpu.VMEM((count, 1), f32),
            pltpu.VMEM((count, 1), f32),
            pltpu.VMEM((count, HD), f32),
            pltpu.VMEM((8, rows, HD), bf16),
            pltpu.VMEM((8, rows, HD), bf16),
            dma((4,)), dma((4,)), dma((4, 4)), dma((4, 4)), dma((4,)), dma((4,)),
            dma((9,)), dma((9,)), dma((7,)), dma((7,)), dma((7,)), dma((7,)), dma((2,)),
        ],
        compiler_params=params(2, vmem_limit_bytes=32 << 20),
        name="attention_layer",
    )(kv, query, starts, tokens, w_out, gain, router, routes)


HALF = 32


def ring_places():
    s, t, plane, z, core, x, y = places()
    across = ((1 - plane) * 16 + z * 2 + core, (1 - x) * 4 + y)
    twin = (s + 1 - 2 * core, t)
    ring = [(plane * 16 + ((z + d) % 8) * 2 + core, t) for d in (1, 7)]
    return s, z, core, [plane, 1 - plane], across, twin, ring


def spread_kernel(
    rows_ref, out_ref, ax_send, ax_recv, az_send, az_recv,
    bx_send, bx_recv, bz_send, bz_recv, c_send, c_recv, local,
):
    s, z, core, planes, across, twin, ring = ring_places()
    greet([across, twin] + ring)
    moves = Copies(twin)
    part_a, part_b = pl.ds(0, HALF), pl.ds(HALF, HALF)
    quarters = [pl.ds(HALF, HALF // 2), pl.ds(HALF + HALF // 2, HALF // 2)]

    def slot(p, way, distance):
        back = (z + 8 - distance) % 8 if way == 0 else (z + distance) % 8
        return planes[p] * 16 + back * 2 + core

    twins = []

    def to_twin(src, block, part):
        k = len(twins)
        twins.append(part)
        moves.start(src, out_ref.at[block, part], c_send.at[k], c_recv.at[k], twin)

    crossed = []

    def cross(src, block):
        k = len(crossed)
        crossed.append(k)
        moves.start(src, out_ref.at[block, part_b], bx_send.at[k], bx_recv.at[k], across)

    def a_travels(p, way, distance):
        return distance <= 3 or (distance == 4 and p == way)

    def a_arrives(p, way, distance):
        if not a_travels(p, way, distance):
            return
        block, k = slot(p, way, distance), distance - 1
        piece = out_ref.at[block, part_a]
        moves.landed(piece, az_send.at[p, way, k], az_recv.at[p, way, k])
        if a_travels(p, way, distance + 1):
            moves.start(piece, piece, az_send.at[p, way, k + 1], az_recv.at[p, way, k + 1], ring[way])
        to_twin(piece, block, part_a)

    def b_arrives(way, distance):
        block, k = slot(0, way, distance), distance - 1
        if distance == 4:
            piece = out_ref.at[block, quarters[way]]
            moves.landed(piece, bz_send.at[way, k], bz_recv.at[way, k])
            if way == 0:
                return
        piece = out_ref.at[block, part_b]
        if distance < 4:
            moves.landed(piece, bz_send.at[way, k], bz_recv.at[way, k])
            onward = out_ref.at[block, quarters[way]] if distance == 3 else piece
            moves.start(onward, onward, bz_send.at[way, k + 1], bz_recv.at[way, k + 1], ring[way])
        cross(piece, block)
        to_twin(piece, block, part_b)

    def b_crossed(k, way, distance):
        block = slot(1, way, distance)
        piece = out_ref.at[block, part_b]
        moves.landed(piece, bx_send.at[k], bx_recv.at[k])
        to_twin(piece, block, part_b)

    own = pltpu.make_async_copy(rows_ref, out_ref.at[s], local)
    own.start()
    own_a, own_b = rows_ref.at[part_a], rows_ref.at[part_b]
    moves.start(own_a, out_ref.at[s, part_a], ax_send, ax_recv, across)
    for way in range(2):
        moves.start(own_b, out_ref.at[s, part_b], bz_send.at[way, 0], bz_recv.at[way, 0], ring[way])
    for way in range(2):
        moves.start(own_a, out_ref.at[s, part_a], az_send.at[0, way, 0], az_recv.at[0, way, 0], ring[way])
    cross(own_b, s)
    to_twin(own_a, s, part_a)
    to_twin(own_b, s, part_b)
    block = across[0]
    piece = out_ref.at[block, part_a]
    moves.landed(piece, ax_send, ax_recv)
    for way in range(2):
        moves.start(piece, piece, az_send.at[1, way, 0], az_recv.at[1, way, 0], ring[way])
    to_twin(piece, block, part_a)
    for distance in range(1, 5):
        for way in range(2):
            b_arrives(way, distance)
        for p in range(2):
            for way in range(2):
                a_arrives(p, way, distance)
        if distance == 1:
            b_crossed(0, 0, 0)
        else:
            b_crossed(2 * distance - 3, 0, distance - 1)
            b_crossed(2 * distance - 2, 1, distance - 1)
    b_crossed(7, 0, 4)
    own.wait()
    for k, part in enumerate(twins):
        moves.landed(out_ref.at[twin[0], part], c_send.at[k], c_recv.at[k])
    moves.drain()


def spread(rows):
    dma = pltpu.SemaphoreType.DMA
    return pl.pallas_call(
        spread_kernel,
        out_shape=jax.ShapeDtypeStruct((32,) + rows.shape, rows.dtype),
        in_specs=[IN_VMEM],
        out_specs=IN_VMEM,
        scratch_shapes=[
            dma(()), dma(()), dma((2, 2, 4)), dma((2, 2, 4)), dma((8,)), dma((8,)),
            dma((2, 4)), dma((2, 4)), dma((32,)), dma((32,)), dma(()),
        ],
        compiler_params=params(4, vmem_limit_bytes=12 << 20),
        name="spread",
    )(rows)


CHUNK = 256


def expert_kernel(rows_ref, gate_ref, up_ref, down_ref, out_ref, column, lane, gathered, contribution, starts):
    width = gate_ref.shape[0]
    blocks = rows_ref.shape[0] // CHUNK
    expert = lax.axis_index("seq")
    bf16, f32 = jnp.bfloat16, jnp.float32
    down_index = lax.broadcasted_iota(jnp.int32, (CHUNK, CHUNK), 0)
    along_index = lax.broadcasted_iota(jnp.int32, (CHUNK, CHUNK), 1)
    zero_first = (((0,), (0,)), ((), ()))

    tokens = rows_ref.shape[0]
    lower, upper, same = [
        test.astype(f32).astype(bf16)
        for test in (along_index <= down_index, down_index <= along_index, down_index == along_index)
    ]
    before = jnp.zeros((1, 1), f32)
    befores = []
    for block in range(blocks):
        routed = (rows_ref[pl.ds(block * CHUNK, CHUNK), width:].astype(f32) != 0.0).astype(f32)
        here = lax.broadcasted_iota(jnp.int32, routed.shape, 1) == expert
        routed = jnp.where(here, routed, 0.0)
        ones = routed.astype(bf16)
        hit = jnp.sum(routed, axis=1, keepdims=True)
        rank = jnp.sum(jnp.dot(lower, ones, preferred_element_type=f32), axis=1, keepdims=True)
        column[pl.ds(block * CHUNK, CHUNK), :] = jnp.where(hit > 0.0, rank + (before - 1.0), -1.0)
        rank = jnp.sum(lax.dot_general(ones, upper, zero_first, preferred_element_type=f32), axis=0, keepdims=True)
        hit = jnp.sum(lax.dot_general(ones, same, zero_first, preferred_element_type=f32), axis=0, keepdims=True)
        lane[:, pl.ds(block * CHUNK, CHUNK)] = jnp.where(hit > 0.0, rank + (before - 1.0), -1.0)
        befores.append(before)
        before = before + jnp.sum(hit, axis=1, keepdims=True)
    for block, count in enumerate(befores + [before]):
        starts[block] = jnp.sum(count).astype(jnp.int32)
    total = starts[blocks]

    def picks_of(base, first, rows):
        slots = base + lax.broadcasted_iota(jnp.int32, (CHUNK, 1), 0)
        return (lane[:, pl.ds(first, rows)] == slots.astype(f32)).astype(f32).astype(bf16)

    def backs_of(base, block):
        slots = base + lax.broadcasted_iota(jnp.int32, (1, CHUNK), 1)
        return (column[pl.ds(block * CHUNK, CHUNK), :] == slots.astype(f32)).astype(f32).astype(bf16)

    def compute(rows, all_gates):
        here = lax.broadcasted_iota(jnp.int32, all_gates.shape, 1) == expert
        gates = jnp.sum(jnp.where(here, all_gates, 0.0), axis=1, keepdims=True)
        rows = rows.astype(bf16)
        gate_out = jnp.dot(rows, gate_ref[...], preferred_element_type=f32)
        up_out = jnp.dot(rows, up_ref[...], preferred_element_type=f32)
        active = (jnp.maximum(gate_out, 0.0) * up_out).astype(bf16)
        down_out = jnp.dot(active, down_ref[...], preferred_element_type=f32) * gates
        contribution[...] = down_out.astype(bf16)

    picks = picks_of(0, 0, tokens)
    compute(
        jnp.dot(picks, rows_ref[:, :width], preferred_element_type=f32),
        jnp.dot(picks, rows_ref[:, width:], preferred_element_type=f32),
    )
    for block in range(blocks):
        placed = jnp.dot(backs_of(0, block), contribution[...], preferred_element_type=f32)
        out_ref[pl.ds(block * CHUNK, CHUNK), :] = placed.astype(bf16)

    def more(number, _):
        base = number * CHUNK
        part = tokens // 4
        gathered[...] = jnp.zeros_like(gathered)
        for first in range(0, tokens, part):
            low, high = starts[first // CHUNK], starts[(first + part) // CHUNK]

            @pl.when((low < base + CHUNK) & (high > base))
            def _():
                gathered[...] += jnp.dot(
                    picks_of(base, first, part), rows_ref[pl.ds(first, part), :], preferred_element_type=f32
                )

        compute(gathered[:, :width], gathered[:, width:])
        for block in range(blocks):

            @pl.when((starts[block] < base + CHUNK) & (starts[block + 1] > base))
            def _():
                span = pl.ds(block * CHUNK, CHUNK)
                placed = jnp.dot(backs_of(base, block), contribution[...], preferred_element_type=f32)
                out_ref[span, :] = (out_ref[span, :].astype(f32) + placed).astype(bf16)

        return 0

    lax.fori_loop(1, (total + CHUNK - 1) // CHUNK, more, 0)


def run_expert(rows, w_gate, w_up, w_down):
    tokens, columns = rows.shape
    width = w_gate.shape[0]
    return pl.pallas_call(
        expert_kernel,
        out_shape=jax.ShapeDtypeStruct((tokens, width), jnp.bfloat16),
        in_specs=[IN_VMEM] * 4,
        out_specs=IN_VMEM,
        scratch_shapes=[
            pltpu.VMEM((tokens, 1), jnp.float32),
            pltpu.VMEM((1, tokens), jnp.float32),
            pltpu.VMEM((CHUNK, columns), jnp.float32),
            pltpu.VMEM((CHUNK, width), jnp.bfloat16),
            pltpu.SMEM((tokens // CHUNK + 1,), jnp.int32),
        ],
        compiler_params=pltpu.CompilerParams(vmem_limit_bytes=28 << 20),
        name="run_expert",
    )(rows, w_gate, w_up, w_down)


def collect_kernel(
    in_ref, out_ref, other, total_a, total_b, a_in, b_in, bx_in, from_x,
    ax_send, ax_recv, az_send, az_recv, bx_send, bx_recv, bz_send, bz_recv, c_send, c_recv,
):
    s, z, core, planes, across, twin, ring = ring_places()
    greet([across, twin] + ring)
    moves = Copies(twin)
    part_a, part_b = pl.ds(0, HALF), pl.ds(HALF, HALF)
    quarters = [pl.ds(0, HALF // 2), pl.ds(HALF // 2, HALF // 2)]
    wide = lambda values: values.astype(jnp.float32)

    def place(p, way, distance):
        ahead = (z + distance) % 8 if way == 0 else (z + 8 - distance) % 8
        return ahead, planes[p] * 8 + ahead

    order = [(1, 0, 4), (0, 0, 4)]
    for distance in (3, 2, 1):
        order += [(p, way, distance) for p in (1, 0) for way in range(2)]
    order += [(1, 0, 0), (0, 0, 0)]
    for k, key in enumerate(order):
        _, i = place(*key)
        moves.start(in_ref.at[2 * i + 1 - core], other.at[i], c_send.at[k], c_recv.at[k], twin)

    crossed = {}
    for k, (p, way, distance) in enumerate(order):
        ahead, i = place(p, way, distance)
        moves.landed(other.at[i], c_send.at[k], c_recv.at[k])

        mine = wide(in_ref[2 * i + core, part_b]) + wide(other[i, part_b])
        if p == 1:
            total_b[i] = mine.astype(jnp.bfloat16)
            j = len(crossed)
            crossed[way, distance] = j
            moves.start(total_b.at[i], bx_in.at[ahead], bx_send.at[j], bx_recv.at[j], across)

        ours = wide(in_ref[2 * i + core, part_a]) + wide(other[i, part_a])
        if distance > 0:
            ways = [p] if distance == 4 else [way]
            for w in ways:
                if distance < (4 if p == w else 3):
                    piece = a_in.at[p, w, distance]
                    moves.landed(piece, az_send.at[p, w, distance], az_recv.at[p, w, distance])
                    ours = ours + wide(piece[...])
                total_a[i] = ours.astype(jnp.bfloat16)
                moves.start(
                    total_a.at[i], a_in.at[p, w, distance - 1],
                    az_send.at[p, w, distance - 1], az_recv.at[p, w, distance - 1], ring[w],
                )
        else:
            for w in range(2):
                piece = a_in.at[p, w, 0]
                moves.landed(piece, az_send.at[p, w, 0], az_recv.at[p, w, 0])
                ours = ours + wide(piece[...])
            if p == 1:
                total_a[i] = ours.astype(jnp.bfloat16)
                moves.start(total_a.at[i], from_x, ax_send, ax_recv, across)

        if p == 0:
            j = crossed[way, distance]
            moves.landed(bx_in.at[ahead], bx_send.at[j], bx_recv.at[j])
            mine = mine + wide(bx_in[ahead])
            if distance == 4:
                total_b[i] = mine.astype(jnp.bfloat16)
                for w in range(2):
                    moves.start(
                        total_b.at[i, quarters[w]], b_in.at[w, 3, quarters[w]],
                        bz_send.at[w, 3], bz_recv.at[w, 3], ring[w],
                    )
            elif distance == 3:
                piece = b_in.at[way, 3, quarters[way]]
                moves.landed(piece, bz_send.at[way, 3], bz_recv.at[way, 3])
                split = HALF // 2
                first, second = mine[:split], mine[split:]
                if way == 0:
                    first = first + wide(piece[...])
                else:
                    second = second + wide(piece[...])
                total_b[i, quarters[0]] = first.astype(jnp.bfloat16)
                total_b[i, quarters[1]] = second.astype(jnp.bfloat16)
            elif distance > 0:
                piece = b_in.at[way, distance]
                moves.landed(piece, bz_send.at[way, distance], bz_recv.at[way, distance])
                total_b[i] = (mine + wide(piece[...])).astype(jnp.bfloat16)
            if 0 < distance < 4:
                moves.start(
                    total_b.at[i], b_in.at[way, distance - 1],
                    bz_send.at[way, distance - 1], bz_recv.at[way, distance - 1], ring[way],
                )
            if distance == 0:
                for w in range(2):
                    piece = b_in.at[w, 0]
                    moves.landed(piece, bz_send.at[w, 0], bz_recv.at[w, 0])
                    mine = mine + wide(piece[...])
                out_ref[part_b, :] = mine.astype(out_ref.dtype)
                moves.landed(from_x, ax_send, ax_recv)
                out_ref[part_a, :] = (ours + wide(from_x[...])).astype(out_ref.dtype)
    moves.drain()


def collect(parts):
    dma = pltpu.SemaphoreType.DMA
    _, rows, width = parts.shape
    vmem = lambda *lead: pltpu.VMEM(lead + (width,), parts.dtype)
    return pl.pallas_call(
        collect_kernel,
        out_shape=jax.ShapeDtypeStruct((rows, width), jnp.bfloat16),
        in_specs=[IN_VMEM],
        out_specs=IN_VMEM,
        scratch_shapes=[
            vmem(16, rows), vmem(16, HALF), vmem(16, HALF), vmem(2, 2, 4, HALF), vmem(2, 4, HALF),
            vmem(8, HALF), vmem(HALF),
            dma(()), dma(()), dma((2, 2, 4)), dma((2, 2, 4)), dma((8,)), dma((8,)),
            dma((2, 4)), dma((2, 4)), dma((16,)), dma((16,)),
        ],
        compiler_params=params(5, vmem_limit_bytes=28 << 20),
        name="collect",
    )(parts)


def on_device(
    tokens, segment_ids, routes, attn_gain, w_query, w_key, w_value, w_out,
    moe_gain, w_router, w_gate, w_up, w_down,
):
    tp_rank = lax.axis_index("tp")
    seq_rank = lax.axis_index("seq")
    tok_dev, width = tokens.shape
    tok_seq = tok_dev * 8
    bf16, f32 = jnp.bfloat16, jnp.float32
    block_first = seq_rank * tok_seq

    seg_row = jnp.pad(segment_ids, (0, HD - tok_dev), constant_values=-1).reshape(1, HD)
    query, keys, values, own_keys, own_values, segs = tp_gather(
        tokens, seg_row, attn_gain[None], w_query, w_key, w_value
    )

    block_index = block_first + jnp.arange(tok_seq, dtype=jnp.int32)
    near = segs[:, :, 0, :tok_dev].reshape(9, tok_seq)
    near_index = block_index[None, :] - tok_seq * jnp.arange(9, dtype=jnp.int32)[:, None]
    labels = jnp.arange(6, dtype=jnp.int32)
    hits = (near[None] == labels[:, None, None]) & (near_index >= 0)[None]
    firsts = jnp.min(jnp.where(hits, near_index[None], 1 << 30), axis=(1, 2))
    starts = jnp.sum(jnp.where(near[0][:, None] == labels[None, :], firsts[None, :], 0), axis=1)
    position = (block_index - starts).astype(f32)
    inverse = ROTARY ** (-(jnp.arange(HD // 2, dtype=f32) * 2.0 / HD))
    angle = position[:, None] * inverse[None, :]
    cosine, sine = jnp.cos(angle), jnp.sin(angle)

    query = rotate(query, cosine, sine).astype(bf16)
    keys = rotate(keys, cosine, sine).astype(bf16)
    own = lambda table: lax.dynamic_slice_in_dim(table, tp_rank * tok_dev, tok_dev, 0)
    own_keys = rotate(own_keys, own(cosine), own(sine)).astype(bf16)
    kv_cache = jnp.stack(
        [jnp.transpose(m.reshape(tok_dev, KVH, HD), (1, 0, 2)) for m in (own_keys, own_values)]
    )
    kv_own = jnp.stack([m.reshape(4, tok_seq // 4, HD) for m in (keys, values)], axis=1)
    resid, payload = attention_layer(
        kv_own, query, starts[:, None], tokens, w_out, moe_gain[None], w_router, routes
    )
    arrived = spread(payload).reshape(32 * tok_dev, width + HD)
    parts = run_expert(arrived, w_gate[0], w_up[0], w_down[0])
    moe = collect(parts.reshape(32, tok_dev, width))
    layer_out = (resid + moe.astype(f32)).astype(bf16)
    return (layer_out, kv_cache)


def solution(mesh):
    placed = (
        P(("seq", "tp"), None),
        P(("seq", "tp")),
        P(("seq", "tp"), None),
        P(),
        P(None, "tp"),
        P(),
        P(),
        P("tp", None),
        P(),
        P(),
        P("seq", None, None),
        P("seq", None, None),
        P("seq", None, None),
    )
    return jax.shard_map(
        on_device,
        mesh=mesh,
        in_specs=placed,
        out_specs=(P(("seq", "tp"), None), P(None, None, ("seq", "tp"), None)),
        check_vma=False,
    )
```
